32 devices in a mesh: ctx: 8 (over z, core), tp: 4 (over y, x).
Axes of the slice: x: 2, y: 2, z: 4, core: 2. Of those that a mesh axis runs over, the one named last changes fastest.
Arguments:
- query_proj: bfloat16 [4096, 8192], P('tp', 'ctx'), may hold values from -6 to 6
- key_proj: bfloat16 [4096, 8192], P('tp', 'ctx'), may hold values from -6 to 6
- value_proj: bfloat16 [4096, 8192], P('tp', 'ctx'), may hold values from -6 to 6
- short_taps: float32 [3, 3, 4096], P(None, None, 'tp'), may hold values from -3.5 to 3.5
- long_filter: float32 [4096, 8192], P(('tp', 'ctx')), may hold values from -0.0625 to 0.0625
- out_weight: bfloat16 [4096, 4096], P('tp'), may hold values from -0.125 to 0.125
- medium_taps: bfloat16 [128, 4096], P(None, 'tp'), may hold values from -0.5 to 0.5
Outputs:
- operator: bfloat16 [4096, 8192], P('tp', 'ctx')
- medium: bfloat16 [4096, 8192], P('tp', 'ctx')
The draws below stay inside these ranges and needn't reach their ends.
All inputs are finite; a program needn't handle non-finite values.
Results may differ from the reference program's by a relative error of at most 0.014.
Values may be sent and summed in bfloat16 or wider, within the bound.
No kernel may reach another device: no remote copies, remote signals or barrier semaphores. Data moves between devices by JAX's collectives and lax.ppermute only.
A program may use at most 320 MiB of HBM per device.

```python
import math
import jax
import jax.numpy as jnp
from jax import lax

D = 4096
MTAPS = 128
STAPS = 3
SEQ = 8192


def strengthened(values, key, source, target, shards_of, factor):
    def block_of(axis_at):
        return (jnp.arange(values.shape[axis_at]) // (values.shape[axis_at] // shards_of)).reshape((-1,) + (1,) * (values.ndim - 1 - axis_at))

    one_side = jax.random.permutation(key, shards_of)[block_of(target)]
    far = (block_of(target) + shards_of // 2) % shards_of
    return jnp.where((block_of(source) == one_side) | (block_of(source) == far), factor * values, values)


def steps_of(rng, dims, split, smallest, high):
    def one(axis_at, blocks):
        heights = jax.random.uniform(jax.random.fold_in(jax.random.fold_in(rng, 6), axis_at), (blocks,), jnp.float32, smallest / len(split), high / len(split))
        return jnp.repeat(jnp.exp(heights), dims[axis_at] // blocks).reshape((-1,) + (1,) * (len(dims) - axis_at - 1))

    gain = one(*split[0])
    for cut in split[1:]:
        gain = gain * one(*cut)
    return gain


def noise(stream_key, shape, deviation, limit, split=(), kind=jnp.bfloat16):
    array = jax.random.normal(stream_key, shape, jnp.float32) * deviation
    if len(split) > 0:
        array = steps_of(stream_key, shape, split, -0.22, 0.18) * array
    return jnp.clip(array, min=-limit, max=limit).astype(kind)


def heavy_noise(rng, shape, scale, limit, cuts, heavy, kind=jnp.bfloat16):
    drawn = scale * jax.random.normal(rng, shape, jnp.float32)
    if cuts:
        drawn = drawn * steps_of(rng, shape, cuts, -0.22, 0.18)
    return jnp.clip(strengthened(drawn, jax.random.fold_in(rng, 3), *heavy), -limit, limit).astype(kind)


def setup_inputs(seed: int = 0) -> dict:
    splits = jax.random.split(jax.random.key(seed), 8)
    return {
        "query_proj": noise(splits[0], (D, SEQ), 1.0, 6.0, ((0, 4), (1, 8))),
        "key_proj": noise(splits[1], (D, SEQ), 1.0, 6.0, ((0, 4), (1, 8))),
        "value_proj": noise(splits[2], (D, SEQ), 1.0, 6.0, ((0, 4), (1, 8))),
        "short_taps": noise(splits[3], (3, STAPS, D), STAPS ** -0.5, 3.5, ((2, 4),), jnp.float32),
        "long_filter": noise(splits[4], (D, SEQ), SEQ ** -0.5, 0.0625, ((0, 32),), jnp.float32),
        "out_weight": heavy_noise(splits[5], (D, D), D ** -0.5, 0.125, ((0, 4),), (0, 1, 4, 2.0)),
        "medium_taps": noise(splits[6], (MTAPS, D), MTAPS ** -0.5, 0.5, ((1, 4),)),
    }


def causal_conv(signal, weights):
    width = weights.shape[0]
    length = signal.shape[1]
    padded = jnp.pad(signal, ((0, 0), (width - 1, 0)))
    summed = jnp.zeros(signal.shape, jnp.float32)
    for offset in range(width):
        summed = summed + weights[offset][:, None] * padded[:, width - 1 - offset:width - 1 - offset + length]
    return summed


def long_block(pieces):
    signal, kernel = pieces
    length = signal.shape[1]
    spectrum = jnp.fft.rfft(signal.astype(jnp.float32), n=2 * length, axis=1)
    response = jnp.fft.rfft(kernel, n=2 * length, axis=1)
    result = jnp.fft.irfft(spectrum * response, n=2 * length, axis=1)[:, :length]
    return result.astype(jnp.bfloat16)


def reference(query_proj, key_proj, value_proj, short_taps, long_filter, out_weight, medium_taps):
    query_conv = causal_conv(query_proj.astype(jnp.float32), short_taps[0])
    key_conv = causal_conv(key_proj.astype(jnp.float32), short_taps[1])
    value_conv = causal_conv(value_proj.astype(jnp.float32), short_taps[2])
    mixed = (key_conv * value_conv).astype(jnp.bfloat16)
    block = math.gcd(D, 256)
    blocked = (mixed.reshape(D // block, block, SEQ), long_filter.reshape(D // block, block, SEQ))
    convolved = lax.map(long_block, blocked).reshape(D, SEQ)
    gating = (query_conv * convolved.astype(jnp.float32)).astype(jnp.bfloat16)
    operator = jnp.dot(out_weight.T, gating, preferred_element_type=jnp.float32).astype(jnp.bfloat16)
    medium = causal_conv(operator.astype(jnp.float32), medium_taps.astype(jnp.float32)).astype(jnp.bfloat16)
    return (operator, medium)
```

```python
import functools
import math

import jax
import jax.numpy as jnp
import numpy as np
from jax import lax
from jax.experimental import pallas as pl
from jax.experimental.pallas import tpu as pltpu
from jax.sharding import PartitionSpec as P

LANES = 128
BF16 = jnp.bfloat16
F32 = jnp.float32


def split_table(table):
    high = np.asarray(table, np.float32).astype(BF16)
    low = (np.asarray(table, np.float64) - high.astype(np.float64)).astype(BF16)
    return high, low


def rotation(rows, cols, period):
    angles = 2.0 * math.pi * np.outer(rows, cols) / period
    return np.cos(angles), np.sin(angles)


@functools.lru_cache
def long_tables(length, groups):
    n1 = length // LANES
    first = np.arange(n1)
    lanes = np.arange(LANES)
    cos1, sin1 = rotation(first + 0.25, first, n1)
    outer = np.concatenate([cos1, -sin1], axis=0)
    back = np.concatenate([cos1.T, -sin1.T], axis=1) / n1
    twist_re, twist_im = rotation(first + 0.25, lanes, length)
    cos2, sin2 = rotation(lanes, lanes, LANES)
    inner = np.block([[cos2, -sin2], [sin2, cos2]])
    inner_back = np.block([[cos2, sin2], [-sin2, cos2]]) / LANES
    per = n1 // groups
    fore, rear = [], []
    for me in range(groups):
        ids = np.concatenate([((me - s) % groups) * per + np.arange(per) for s in range(groups)])
        out = np.concatenate([((me + s) % groups) * per + np.arange(per) for s in range(groups)])
        high, low = split_table(outer[:, ids])
        fore.append(np.concatenate([high, low], axis=1))
        high, low = split_table(back[out])
        rear.append(np.concatenate([high, low], axis=1))
    high, low = split_table(outer)
    plain = np.concatenate([high, high, low], axis=1)
    twist = np.stack([twist_re, -twist_im]).astype(np.float32)
    inner_high, inner_low = split_table(inner)
    return dict(
        fore=np.stack(fore),
        rear=np.stack(rear),
        plain=plain,
        twist=twist,
        inner=inner_high,
        inner_low=inner_low,
        inner_back=split_table(inner_back)[0],
    )


@functools.lru_cache
def medium_tables(width):
    span = 2 * width
    cos, sin = rotation(np.arange(span), np.arange(width) + 0.5, span)
    high, low = split_table(np.concatenate([cos, -sin], axis=1))
    last = slice(width, span)
    back = np.concatenate([cos[last].T, -sin[last].T], axis=0) / width
    return high, low, split_table(back)[0]


def dot(left, right):
    return jnp.dot(left, right, preferred_element_type=F32)


def short_conv(block, edge, taps):
    lane = lax.broadcasted_iota(jnp.int32, block.shape, 1)
    older, newer = edge[:, 0:1], edge[:, 1:2]
    back1 = jnp.where(lane == 0, newer, pltpu.roll(block, 1, 1))
    back2 = jnp.where(lane == 0, older, jnp.where(lane == 1, newer, pltpu.roll(block, 2, 1)))
    return taps[:, 0:1] * block + taps[:, 1:2] * back1 + taps[:, 2:3] * back2


def mix_kernel(ids_ref, key_ref, value_ref, aux_ref, out_ref):
    aux = aux_ref[...]
    keys = short_conv(key_ref[...].astype(F32), aux[:, 11:13], aux[:, 3:6])
    values = short_conv(value_ref[...].astype(F32), aux[:, 13:15], aux[:, 6:9])
    mixed = (keys * values).astype(BF16)
    for j in range(out_ref.shape[0]):
        out_ref[j] = mixed[:, j * LANES : (j + 1) * LANES]


def mix(ids, key_proj, value_proj, aux, step, groups):
    channels, tokens = key_proj.shape
    rows = channels // groups
    where = lambda i, ids: (lax.rem(ids[0] + step, groups), 0)
    return pl.pallas_call(
        mix_kernel,
        out_shape=jax.ShapeDtypeStruct((tokens // LANES, rows, LANES), BF16),
        grid_spec=pltpu.PrefetchScalarGridSpec(
            num_scalar_prefetch=1,
            grid=(1,),
            in_specs=[
                pl.BlockSpec((rows, tokens), where),
                pl.BlockSpec((rows, tokens), where),
                pl.BlockSpec((rows, aux.shape[1]), where),
            ],
            out_specs=pl.BlockSpec((tokens // LANES, rows, LANES), lambda i, ids: (0, 0, 0)),
        ),
        name="mix",
    )(ids, key_proj, value_proj, aux)


def twisted(wide, twist_re, twist_im, count):
    half = wide.shape[0] // 2
    out = []
    for c in range(count):
        re = wide[:half, c * LANES : (c + 1) * LANES]
        im = wide[half:, c * LANES : (c + 1) * LANES]
        out.append((re * twist_re - im * twist_im, re * twist_im + im * twist_re))
    return out


def filter_kernel(filter_ref, plain_ref, twist_ref, inner_ref, inner_low_ref, out_ref, rows_ref):
    block = filter_ref.shape[0]
    n1 = filter_ref.shape[1] // LANES
    for n in range(n1):
        rows_ref[n * block : (n + 1) * block, :] = filter_ref[:, n * LANES : (n + 1) * LANES]

    def body(pair, carry):
        loaded = [rows_ref[pl.ds(2 * pair + c, n1, stride=block), :] for c in range(2)]
        both = jnp.concatenate(loaded, axis=1)
        high = both.astype(BF16)
        low = (both - high.astype(F32)).astype(BF16)
        wide = dot(plain_ref[...], jnp.concatenate([high, low, high], axis=0))
        for c, (re, im) in enumerate(twisted(wide, twist_ref[0], twist_ref[1], 2)):
            line = jnp.concatenate([re, im], axis=1)
            high = line.astype(BF16)
            low = (line - high.astype(F32)).astype(BF16)
            out_ref[2 * pair + c] = (
                dot(high, inner_ref[...]) + dot(low, inner_ref[...]) + dot(high, inner_low_ref[...])
            )
        return carry

    lax.fori_loop(0, block // 2, body, 0)


def whole(shape):
    return pl.BlockSpec(shape, lambda *_: (0,) * len(shape))


def spectra(long_filter, tables, block):
    channels, length = long_filter.shape
    n1 = length // LANES
    names = ("plain", "twist", "inner", "inner_low")
    return pl.pallas_call(
        filter_kernel,
        out_shape=jax.ShapeDtypeStruct((channels, n1, 2 * LANES), F32),
        grid=(channels // block,),
        in_specs=[pl.BlockSpec((block, length), lambda i: (i, 0))]
        + [whole(tables[name].shape) for name in names],
        out_specs=pl.BlockSpec((block, n1, 2 * LANES), lambda i: (i, 0, 0)),
        scratch_shapes=[pltpu.VMEM((n1 * block, LANES), F32)],
        name="spectra",
    )(long_filter, *[tables[name] for name in names])


def conv_kernel(groups, ids_ref, *refs):
    pieces = refs[:groups]
    spec_ref, fore_ref, rear_ref, twist_ref, inner_ref, back_ref = refs[groups : groups + 6]
    outs = refs[groups + 6 : 2 * groups + 6]
    rows_ref, done_ref = refs[2 * groups + 6 :]
    per, block, _ = pieces[0].shape
    n1 = groups * per
    for s in range(groups):
        part = pieces[s][...].astype(F32)
        rows_ref[s * per * block : (s + 1) * per * block, :] = part.reshape(per * block, LANES)
    group = math.gcd(block, 8)

    def body(at, carry):
        base = at * group
        lines = []
        for pair in range(group // 2):
            loaded = [
                rows_ref[pl.ds(base + 2 * pair + c, n1, stride=block), :].astype(BF16)
                for c in range(2)
            ]
            both = jnp.concatenate(loaded, axis=1)
            wide = dot(fore_ref[0], jnp.concatenate([both, both], axis=0))
            for re, im in twisted(wide, twist_ref[0], twist_ref[1], 2):
                lines.append(jnp.concatenate([re.astype(BF16), im.astype(BF16)], axis=1))
        spectrum = dot(jnp.concatenate(lines, axis=0), inner_ref[...])
        other = spec_ref[pl.ds(base, group)].reshape(group * n1, 2 * LANES)
        sig_re, sig_im = spectrum[:, :LANES], spectrum[:, LANES:]
        ker_re, ker_im = other[:, :LANES], other[:, LANES:]
        product = jnp.concatenate(
            [
                (sig_re * ker_re - sig_im * ker_im).astype(BF16),
                (sig_re * ker_im + sig_im * ker_re).astype(BF16),
            ],
            axis=1,
        )
        turned = dot(product, back_ref[...])
        for pair in range(group // 2):
            stacks = []
            for c in range(2):
                at_row = (2 * pair + c) * n1
                re = turned[at_row : at_row + n1, :LANES]
                im = turned[at_row : at_row + n1, LANES:]
                top = (re * twist_ref[0] + im * twist_ref[1]).astype(BF16)
                low = (im * twist_ref[0] - re * twist_ref[1]).astype(BF16)
                stacks.append(jnp.concatenate([top, low, top, low], axis=0))
            result = dot(rear_ref[0], jnp.concatenate(stacks, axis=1))
            for c in range(2):
                done_ref[pl.ds(base + 2 * pair + c, n1, stride=block), :] = result[
                    :, c * LANES : (c + 1) * LANES
                ]
        return carry

    lax.fori_loop(0, block // group, body, 0)
    for s in range(groups):
        part = done_ref[s * per * block : (s + 1) * per * block, :]
        outs[s][...] = part.reshape(per, block, LANES).astype(BF16)


def long_conv(ids, pieces, spec, tables, block):
    groups = len(pieces)
    per, channels, _ = pieces[0].shape
    n1 = groups * per
    piece = pl.BlockSpec((per, block, LANES), lambda i, ids: (0, i, 0))
    mine = lambda shape: pl.BlockSpec((1,) + shape[1:], lambda i, ids: (ids[0], 0, 0))
    return pl.pallas_call(
        functools.partial(conv_kernel, groups),
        out_shape=[jax.ShapeDtypeStruct((per, channels, LANES), BF16)] * groups,
        grid_spec=pltpu.PrefetchScalarGridSpec(
            num_scalar_prefetch=1,
            grid=(channels // block,),
            in_specs=[piece] * groups
            + [
                pl.BlockSpec((block, n1, 2 * LANES), lambda i, ids: (i, 0, 0)),
                mine(tables["fore"].shape),
                mine(tables["rear"].shape),
                whole(tables["twist"].shape),
                whole(tables["inner"].shape),
                whole(tables["inner_back"].shape),
            ],
            out_specs=[piece] * groups,
            scratch_shapes=[pltpu.VMEM((n1 * block, LANES), F32)] * 2,
        ),
        name="conv",
    )(
        ids,
        *pieces,
        spec,
        tables["fore"],
        tables["rear"],
        tables["twist"],
        tables["inner"],
        tables["inner_back"],
    )


def project_kernel(groups, ids_ref, *refs):
    pieces = refs[:groups]
    query_ref, aux_ref, weight_ref, left_ref, right_ref, gating_ref = refs[groups:]
    per, rows, _ = pieces[0].shape
    tokens = per * LANES

    @pl.when((pl.program_id(0) == 0) & (pl.program_id(1) == 0))
    def _():
        for s in range(groups):
            at = pl.ds(pl.multiple_of(lax.rem(ids_ref[0] + groups - s, groups) * rows, rows), rows)
            aux = aux_ref[at, :]
            query = short_conv(query_ref[at, :].astype(F32), aux[:, 9:11], aux[:, 0:3])
            conv = jnp.concatenate([pieces[s][j].astype(F32) for j in range(per)], axis=1)
            gating_ref[at, :] = (query * conv).astype(BF16)

    out = lax.dot_general(
        weight_ref[...], gating_ref[...], (((0,), (0,)), ((), ())), preferred_element_type=F32
    ).astype(BF16)
    left_ref[0] = out[:, : tokens // 2]
    right_ref[0] = out[:, tokens // 2 :]


def project(ids, pieces, query_proj, aux, out_weight, shards_count, swap):
    groups = len(pieces)
    per, rows, _ = pieces[0].shape
    channels, tokens = query_proj.shape
    width = out_weight.shape[1] // shards_count
    step = min(width, 512)
    inner = width // step
    target = (lambda r, ids: ids[1] ^ r) if swap else (lambda r, ids: r)
    left_at = (lambda r: (1 - (r & 1)) * 2 + (r >> 1)) if swap else (lambda r: r)
    right_at = (lambda r: (1 - (r >> 1)) * 2 + (r & 1)) if swap else (lambda r: r)
    half = jax.ShapeDtypeStruct((shards_count, width, tokens // 2), BF16)
    block = (1, step, tokens // 2)
    return pl.pallas_call(
        functools.partial(project_kernel, groups),
        out_shape=[half, half],
        grid_spec=pltpu.PrefetchScalarGridSpec(
            num_scalar_prefetch=1,
            grid=(shards_count, inner),
            in_specs=[whole((per, rows, LANES))] * groups
            + [
                whole((channels, tokens)),
                whole(aux.shape),
                pl.BlockSpec((channels, step), lambda r, h, ids: (0, target(r, ids) * inner + h)),
            ],
            out_specs=[
                pl.BlockSpec(block, lambda r, h, ids: (left_at(r), h, 0)),
                pl.BlockSpec(block, lambda r, h, ids: (right_at(r), h, 0)),
            ],
            scratch_shapes=[pltpu.VMEM((channels, tokens), BF16)],
        ),
        name="project",
    )(ids, *pieces, query_proj, aux, out_weight)


def medium_kernel(left_ref, right_ref, edge_ref, taps_ref, fore_ref, low_ref, back_ref, *outs):
    oper_ref, out_ref = outs
    width = taps_ref.shape[0]
    over_taps = (((0,), (0,)), ((), ()))
    taps = taps_ref[...]
    spec = lax.dot_general(taps, fore_ref[:width], over_taps, preferred_element_type=F32)
    spec = spec + lax.dot_general(taps, low_ref[:width], over_taps, preferred_element_type=F32)
    ker_re, ker_im = spec[:, :width], spec[:, width:]
    value = jnp.concatenate([left_ref[...], right_ref[...]], axis=1)
    oper_ref[...] = value
    wide = jnp.concatenate([edge_ref[...], value], axis=1)
    for b in range(value.shape[1] // width):
        window = wide[:, b * width : (b + 2) * width]
        sig = dot(window, fore_ref[...]) + dot(window, low_ref[...])
        sig_re, sig_im = sig[:, :width], sig[:, width:]
        product = jnp.concatenate(
            [
                (sig_re * ker_re - sig_im * ker_im).astype(BF16),
                (sig_re * ker_im + sig_im * ker_re).astype(BF16),
            ],
            axis=1,
        )
        out_ref[:, b * width : (b + 1) * width] = dot(product, back_ref[...]).astype(BF16)


def medium(left, right, edge, taps, tables):
    channels, half = left.shape
    width = taps.shape[0]
    block = min(channels, 256)
    row = lambda n: pl.BlockSpec((block, n), lambda i: (i, 0))
    full = jax.ShapeDtypeStruct((channels, 2 * half), BF16)
    return pl.pallas_call(
        medium_kernel,
        out_shape=[full, full],
        grid=(channels // block,),
        in_specs=[
            row(half),
            row(half),
            row(width),
            pl.BlockSpec((width, block), lambda i: (0, i)),
        ]
        + [whole(t.shape) for t in tables],
        out_specs=[row(2 * half)] * 2,
        name="medium",
    )(left, right, edge, taps, *tables)


def ring(block, axis, distance):
    count = lax.axis_size(axis)
    return lax.ppermute(block, axis, [(i, (i + distance) % count) for i in range(count)])


def forward(block, axis):
    count = lax.axis_size(axis)
    return lax.ppermute(block, axis, [(i, i + 1) for i in range(count - 1)])


def swapped(block, axis, bit):
    return lax.ppermute(block, axis, [(i, i ^ bit) for i in range(lax.axis_size(axis))])


def reduced(left, right, swap):
    if not swap:
        both = [
            lax.psum_scatter(v, "tp", scatter_dimension=0, tiled=True)[0] for v in (left, right)
        ]
        return both
    got_left = swapped(left[:2], "tp", 1)
    got_right = swapped(right[:2], "tp", 2)
    left = (left[2:].astype(F32) + got_left.astype(F32)).astype(BF16)
    right = (right[2:].astype(F32) + got_right.astype(F32)).astype(BF16)
    got_left = swapped(left[1], "tp", 2)
    got_right = swapped(right[1], "tp", 1)
    left = (left[0].astype(F32) + got_left.astype(F32)).astype(BF16)
    right = (right[0].astype(F32) + got_right.astype(F32)).astype(BF16)
    return left, right


def shards(query_proj, key_proj, value_proj, short_taps, long_filter, out_weight, medium_taps):
    channels, tokens = query_proj.shape
    groups = lax.axis_size("ctx")
    parts = lax.axis_size("tp")
    swap = parts == 4
    length = long_filter.shape[1]
    tables = long_tables(length, groups)
    ids = jnp.stack([lax.axis_index("ctx"), lax.axis_index("tp")]).astype(jnp.int32)
    tails = [x[:, -2:] for x in (query_proj, key_proj, value_proj)]
    edges = forward(jnp.concatenate(tails, axis=1), "ctx").astype(F32)
    flat_taps = short_taps.reshape(9, channels).T
    aux = jnp.concatenate([flat_taps, edges, jnp.zeros((channels, 1), F32)], axis=1)
    owned = long_filter.shape[0]
    spec = spectra(long_filter, tables, min(owned, 16))
    sent = [mix(ids, key_proj, value_proj, aux, s, groups) for s in range(groups)]
    pieces = [sent[0]] + [ring(sent[s], "ctx", s) for s in range(1, groups)]
    results = long_conv(ids, pieces, spec, tables, min(owned, 32))
    back = [results[0]] + [ring(results[s], "ctx", s) for s in range(1, groups)]
    left, right = project(ids, back, query_proj, aux, out_weight, parts, swap)
    left, right = reduced(left, right, swap)
    width = medium_taps.shape[0]
    edge = forward(right[:, -width:], "ctx")
    operator, result = medium(left, right, edge, medium_taps, medium_tables(width))
    return (operator, result)


def solution(mesh):
    in_specs = (
        P("tp", "ctx"),
        P("tp", "ctx"),
        P("tp", "ctx"),
        P(None, None, "tp"),
        P(("tp", "ctx"), None),
        P("tp", None),
        P(None, "tp"),
    )
    out_specs = (P("tp", "ctx"), P("tp", "ctx"))
    return jax.shard_map(shards, mesh=mesh, in_specs=in_specs, out_specs=out_specs, check_vma=False)
```

```python
import functools
import math

import jax
import jax.numpy as jnp
import numpy as np
from jax import lax
from jax.experimental import pallas as pl
from jax.experimental.pallas import tpu as pltpu
from jax.sharding import PartitionSpec as P


LANES = 128
BF16 = jnp.bfloat16
F32 = jnp.float32


def split_table(table):
    high = np.asarray(table, np.float32).astype(BF16)
    low = (np.asarray(table, np.float64) - high.astype(np.float64)).astype(BF16)
    return high, low


def rotation(rows, cols, period):
    angles = 2.0 * math.pi * np.outer(rows, cols) / period
    return np.cos(angles), np.sin(angles)


@functools.lru_cache
def long_tables(length, groups):
    n1 = length // LANES
    first = np.arange(n1)
    lanes = np.arange(LANES)
    cos1, sin1 = rotation(first + 0.25, first, n1)
    outer = np.concatenate([cos1, -sin1], axis=0)
    back = np.concatenate([cos1.T, -sin1.T], axis=1) / n1
    twist_re, twist_im = rotation(first + 0.25, lanes, length)
    cos2, sin2 = rotation(lanes, lanes, LANES)
    inner = np.block([[cos2, -sin2], [sin2, cos2]])
    inner_back = np.block([[cos2, sin2], [-sin2, cos2]]) / LANES
    per = n1 // groups
    fore, rear = [], []
    for me in range(groups):
        ids = np.concatenate([((me - s) % groups) * per + np.arange(per) for s in range(groups)])
        out = np.concatenate([((me + s) % groups) * per + np.arange(per) for s in range(groups)])
        high, low = split_table(outer[:, ids])
        fore.append(np.concatenate([high, low], axis=1))
        high, low = split_table(back[out])
        rear.append(np.concatenate([high, low], axis=1))
    high, low = split_table(outer)
    plain = np.concatenate([high, high, low], axis=1)
    twist = np.stack([twist_re, -twist_im]).astype(np.float32)
    inner_high, inner_low = split_table(inner)
    return dict(
        fore=np.stack(fore),
        rear=np.stack(rear),
        plain=plain,
        twist=twist,
        inner=inner_high,
        inner_low=inner_low,
        inner_back=split_table(inner_back)[0],
    )


@functools.lru_cache
def medium_tables(width):
    span = 2 * width
    cos, sin = rotation(np.arange(span), np.arange(width) + 0.5, span)
    high, low = split_table(np.concatenate([cos, -sin], axis=1))
    last = slice(width, span)
    back = np.concatenate([cos[last].T, -sin[last].T], axis=0) / width
    return high, low, split_table(back)[0]


def grant(mib):
    return pltpu.CompilerParams(vmem_limit_bytes=mib * 1024 * 1024)


def dot(left, right):
    return jnp.dot(left, right, preferred_element_type=F32)


def short_conv(block, edge, taps):
    lane = lax.broadcasted_iota(jnp.int32, block.shape, 1)
    older, newer = edge[:, 0:1], edge[:, 1:2]
    back1 = jnp.where(lane == 0, newer, pltpu.roll(block, 1, 1))
    back2 = jnp.where(lane == 0, older, jnp.where(lane == 1, newer, pltpu.roll(block, 2, 1)))
    return taps[:, 0:1] * block + taps[:, 1:2] * back1 + taps[:, 2:3] * back2


def mix_kernel(ids_ref, key_ref, value_ref, aux_ref, *out_refs):
    aux = aux_ref[...]
    keys = short_conv(key_ref[...].astype(F32), aux[:, 11:13], aux[:, 3:6])
    values = short_conv(value_ref[...].astype(F32), aux[:, 13:15], aux[:, 6:9])
    mixed = (keys * values).astype(BF16)
    for at, out_ref in enumerate(out_refs):

        @pl.when(pl.program_id(0) == at)
        def _():
            for j in range(out_ref.shape[0]):
                out_ref[j] = mixed[:, j * LANES : (j + 1) * LANES]


def mix(ids, key_proj, value_proj, aux, first, count, groups):
    channels, tokens = key_proj.shape
    rows = channels // groups
    where = lambda i, ids: (lax.rem(ids[0] + first + i, groups), 0)
    piece = (tokens // LANES, rows, LANES)
    return pl.pallas_call(
        mix_kernel,
        out_shape=[jax.ShapeDtypeStruct(piece, BF16)] * count,
        grid_spec=pltpu.PrefetchScalarGridSpec(
            num_scalar_prefetch=1,
            grid=(count,),
            in_specs=[
                pl.BlockSpec((rows, tokens), where),
                pl.BlockSpec((rows, tokens), where),
                pl.BlockSpec((rows, aux.shape[1]), where),
            ],
            out_specs=[whole(piece)] * count,
        ),
        compiler_params=grant(12),
        name="mix",
    )(ids, key_proj, value_proj, aux)


def twisted(wide, twist_re, twist_im, count):
    half = wide.shape[0] // 2
    out = []
    for c in range(count):
        re = wide[:half, c * LANES : (c + 1) * LANES]
        im = wide[half:, c * LANES : (c + 1) * LANES]
        out.append((re * twist_re - im * twist_im, re * twist_im + im * twist_re))
    return out


def filter_kernel(filter_ref, plain_ref, twist_ref, inner_ref, inner_low_ref, out_ref, rows_ref):
    block = filter_ref.shape[0]
    n1 = filter_ref.shape[1] // LANES
    for n in range(n1):
        rows_ref[n * block : (n + 1) * block, :] = filter_ref[:, n * LANES : (n + 1) * LANES]

    group = math.gcd(block, 8)

    def body(at, carry):
        base = at * group
        highs, lows = [], []
        for pair in range(group // 2):
            loaded = [
                rows_ref[pl.ds(base + 2 * pair + c, n1, stride=block), :] for c in range(2)
            ]
            both = jnp.concatenate(loaded, axis=1)
            high = both.astype(BF16)
            low = (both - high.astype(F32)).astype(BF16)
            wide = dot(plain_ref[...], jnp.concatenate([high, low, high], axis=0))
            for re, im in twisted(wide, twist_ref[0], twist_ref[1], 2):
                line = jnp.concatenate([re, im], axis=1)
                high = line.astype(BF16)
                highs.append(high)
                lows.append((line - high.astype(F32)).astype(BF16))
        high = jnp.concatenate(highs, axis=0)
        low = jnp.concatenate(lows, axis=0)
        spectrum = (
            dot(high, inner_ref[...]) + dot(low, inner_ref[...]) + dot(high, inner_low_ref[...])
        )
        out_ref[pl.ds(base, group)] = spectrum.reshape(group, n1, 2 * LANES)
        return carry

    lax.fori_loop(0, block // group, body, 0)


def whole(shape):
    return pl.BlockSpec(shape, lambda *_: (0,) * len(shape))


def spectra(long_filter, tables, block):
    channels, length = long_filter.shape
    n1 = length // LANES
    names = ("plain", "twist", "inner", "inner_low")
    return pl.pallas_call(
        filter_kernel,
        out_shape=jax.ShapeDtypeStruct((channels, n1, 2 * LANES), F32),
        grid=(channels // block,),
        in_specs=[pl.BlockSpec((block, length), lambda i: (i, 0))]
        + [whole(tables[name].shape) for name in names],
        out_specs=pl.BlockSpec((block, n1, 2 * LANES), lambda i: (i, 0, 0)),
        scratch_shapes=[pltpu.VMEM((n1 * block, LANES), F32)],
        compiler_params=grant(20),
        name="spectra",
    )(long_filter, *[tables[name] for name in names])


def conv_kernel(groups, ids_ref, *refs):
    pieces = refs[:groups]
    spec_ref, fore_ref, rear_ref, twist_ref, inner_ref, back_ref = refs[groups : groups + 6]
    outs = refs[groups + 6 : 3 * groups + 6]
    rows_ref, done_ref = refs[3 * groups + 6 :]
    per, block, _ = pieces[0].shape
    n1 = groups * per
    for s in range(groups):
        part = pieces[s][...].astype(F32)
        rows_ref[s * per * block : (s + 1) * per * block, :] = part.reshape(per * block, LANES)
    group = math.gcd(block, 8)

    def body(at, carry):
        base = at * group
        lines = []
        for pair in range(group // 2):
            loaded = [
                rows_ref[pl.ds(base + 2 * pair + c, n1, stride=block), :].astype(BF16)
                for c in range(2)
            ]
            both = jnp.concatenate(loaded, axis=1)
            wide = dot(fore_ref[0], jnp.concatenate([both, both], axis=0))
            for re, im in twisted(wide, twist_ref[0], twist_ref[1], 2):
                lines.append(jnp.concatenate([re.astype(BF16), im.astype(BF16)], axis=1))
        spectrum = dot(jnp.concatenate(lines, axis=0), inner_ref[...])
        other = spec_ref[pl.ds(base, group)].reshape(group * n1, 2 * LANES)
        sig_re, sig_im = spectrum[:, :LANES], spectrum[:, LANES:]
        ker_re, ker_im = other[:, :LANES], other[:, LANES:]
        product = jnp.concatenate(
            [
                (sig_re * ker_re - sig_im * ker_im).astype(BF16),
                (sig_re * ker_im + sig_im * ker_re).astype(BF16),
            ],
            axis=1,
        )
        turned = dot(product, back_ref[...])
        for pair in range(group // 2):
            stacks = []
            for c in range(2):
                at_row = (2 * pair + c) * n1
                re = turned[at_row : at_row + n1, :LANES]
                im = turned[at_row : at_row + n1, LANES:]
                top = (re * twist_ref[0] + im * twist_ref[1]).astype(BF16)
                low = (im * twist_ref[0] - re * twist_ref[1]).astype(BF16)
                stacks.append(jnp.concatenate([top, low, top, low], axis=0))
            result = dot(rear_ref[0], jnp.concatenate(stacks, axis=1))
            for c in range(2):
                done_ref[pl.ds(base + 2 * pair + c, n1, stride=block), :] = result[
                    :, c * LANES : (c + 1) * LANES
                ]
        return carry

    lax.fori_loop(0, block // group, body, 0)
    half = per // 2 * block
    for s in range(2 * groups):
        part = done_ref[s * half : (s + 1) * half, :]
        outs[s][...] = part.reshape(per // 2, block, LANES).astype(BF16)


def long_conv(ids, pieces, spec, tables, block):
    groups = len(pieces)
    per, channels, _ = pieces[0].shape
    n1 = groups * per
    piece = pl.BlockSpec((per, block, LANES), lambda i, ids: (0, i, 0))
    part = pl.BlockSpec((per // 2, block, LANES), lambda i, ids: (0, i, 0))
    mine = lambda shape: pl.BlockSpec((1,) + shape[1:], lambda i, ids: (ids[0], 0, 0))
    return pl.pallas_call(
        functools.partial(conv_kernel, groups),
        out_shape=[jax.ShapeDtypeStruct((per // 2, channels, LANES), BF16)] * (2 * groups),
        grid_spec=pltpu.PrefetchScalarGridSpec(
            num_scalar_prefetch=1,
            grid=(channels // block,),
            in_specs=[piece] * groups
            + [
                pl.BlockSpec((block, n1, 2 * LANES), lambda i, ids: (i, 0, 0)),
                mine(tables["fore"].shape),
                mine(tables["rear"].shape),
                whole(tables["twist"].shape),
                whole(tables["inner"].shape),
                whole(tables["inner_back"].shape),
            ],
            out_specs=[part] * (2 * groups),
            scratch_shapes=[pltpu.VMEM((n1 * block, LANES), F32)] * 2,
        ),
        compiler_params=grant(24),
        name="conv",
    )(
        ids,
        *pieces,
        spec,
        tables["fore"],
        tables["rear"],
        tables["twist"],
        tables["inner"],
        tables["inner_back"],
    )


def query_kernel(query_ref, aux_ref, out_ref):
    aux = aux_ref[...]
    query = short_conv(query_ref[...].astype(F32), aux[:, 9:11], aux[:, 0:3])
    for j in range(out_ref.shape[0]):
        out_ref[j] = query[:, j * LANES : (j + 1) * LANES]


def query_conv(query_proj, aux):
    channels, tokens = query_proj.shape
    block = min(channels, 128)
    count = tokens // LANES
    return pl.pallas_call(
        query_kernel,
        out_shape=jax.ShapeDtypeStruct((count, channels, LANES), F32),
        grid=(channels // block,),
        in_specs=[
            pl.BlockSpec((block, tokens), lambda i: (i, 0)),
            pl.BlockSpec((block, aux.shape[1]), lambda i: (i, 0)),
        ],
        out_specs=pl.BlockSpec((count, block, LANES), lambda i: (0, i, 0)),
        compiler_params=grant(12),
        name="query",
    )(query_proj, aux)


def gate_kernel(groups, ids_ref, *refs):
    pieces = refs[:groups]
    query_ref, left_ref, right_ref = refs[groups:]
    rows = pieces[0].shape[1]
    half = pl.num_programs(0) // 2
    for side, out_ref in enumerate((left_ref, right_ref)):

        @pl.when(pl.program_id(0) // half == side)
        def _():
            for s in range(groups):
                group = lax.rem(ids_ref[0] + groups - s, groups)
                at = pl.ds(pl.multiple_of(group * rows, rows), rows)
                out_ref[at, :] = (query_ref[0, at, :] * pieces[s][0].astype(F32)).astype(BF16)


def gate(ids, pieces, query, start):
    groups = len(pieces)
    per, rows, _ = pieces[0].shape
    channels = query.shape[1]
    half = per // 2
    shape = jax.ShapeDtypeStruct((channels, half * LANES), BF16)
    return pl.pallas_call(
        functools.partial(gate_kernel, groups),
        out_shape=[shape] * 2,
        grid_spec=pltpu.PrefetchScalarGridSpec(
            num_scalar_prefetch=1,
            grid=(per,),
            in_specs=[pl.BlockSpec((1, rows, LANES), lambda j, ids: (j, 0, 0))] * groups
            + [pl.BlockSpec((1, channels, LANES), lambda j, ids: (start + j, 0, 0))],
            out_specs=[
                pl.BlockSpec((channels, LANES), lambda j, ids: (0, jnp.minimum(j, half - 1))),
                pl.BlockSpec((channels, LANES), lambda j, ids: (0, jnp.maximum(j - half, 0))),
            ],
        ),
        compiler_params=grant(12),
        name="gate",
    )(ids, *pieces, query)


def turn_kernel(ids_ref, weight_ref, *out_refs):
    for at, out_ref in enumerate(out_refs):

        @pl.when(pl.program_id(0) == at)
        def _():
            out_ref[...] = weight_ref[...].T


def turned(ids, out_weight, width, shards_of):
    channels = out_weight.shape[0]
    step = min(width, 256)
    inner = width // step
    count = len(shards_of)

    def from_at(k, h, ids):
        shard = shards_of[0](ids)
        for at in range(1, count):
            shard = jnp.where(k == at, shards_of[at](ids), shard)
        return (0, shard * inner + h)

    def out_at(mine):
        return lambda k, h, ids: (
            jnp.where(k == mine, h, jnp.where(k < mine, 0, inner - 1)),
            0,
        )

    return pl.pallas_call(
        turn_kernel,
        out_shape=[jax.ShapeDtypeStruct((width, channels), BF16)] * count,
        grid_spec=pltpu.PrefetchScalarGridSpec(
            num_scalar_prefetch=1,
            grid=(count, inner),
            in_specs=[pl.BlockSpec((channels, step), from_at)],
            out_specs=[pl.BlockSpec((step, channels), out_at(at)) for at in range(count)],
        ),
        compiler_params=grant(12),
        name="turn",
    )(ids, out_weight)


def project_kernel(slot, ids_ref, *refs):
    sources, weights = refs[0:4], refs[4:6]
    sides = refs[6:8], refs[8:10]
    outs = refs[10:12]
    for colour in range(2):
        for partner in range(2):

            @pl.when((pl.program_id(0) == colour) & (((ids_ref[0] & 1) ^ slot) == partner))
            def _():
                out = dot(weights[colour][...], sources[colour][...]) + dot(
                    sides[colour][partner][...], sources[2 + colour][...]
                )
                outs[colour][...] = out.astype(BF16)


def project(ids, own, near, weights, sides, slot):
    width, channels = weights[0].shape
    tokens = own[0].shape[1]
    step = min(width, 512)
    inner = width // step

    def when(active, mine, colour, h):
        return (jnp.where(active, h, jnp.where(colour > mine, inner - 1, 0)), 0)

    def side_at(mine, partner):
        def at(colour, h, ids):
            chosen = ((ids[0] & 1) ^ slot) == partner
            return when((colour == mine) & chosen, mine, jnp.where(chosen, colour, mine), h)

        return at

    def colour_at(mine):
        return lambda colour, h, ids: when(colour == mine, mine, colour, h)

    return pl.pallas_call(
        functools.partial(project_kernel, slot),
        out_shape=[jax.ShapeDtypeStruct((width, tokens), BF16)] * 2,
        grid_spec=pltpu.PrefetchScalarGridSpec(
            num_scalar_prefetch=1,
            grid=(2, inner),
            in_specs=[whole((channels, tokens))] * 4
            + [pl.BlockSpec((step, channels), colour_at(colour)) for colour in range(2)]
            + [
                pl.BlockSpec((step, channels), side_at(colour, partner))
                for colour in range(2)
                for partner in range(2)
            ],
            out_specs=[pl.BlockSpec((step, tokens), colour_at(colour)) for colour in range(2)],
        ),
        compiler_params=grant(20),
        name="project",
    )(ids, *own, *near, *weights, *sides[0], *sides[1])


def medium_spectrum(taps, fore_ref, low_ref):
    width = taps.shape[0]
    over_taps = (((0,), (0,)), ((), ()))
    spec = lax.dot_general(taps, fore_ref[:width], over_taps, preferred_element_type=F32)
    spec = spec + lax.dot_general(taps, low_ref[:width], over_taps, preferred_element_type=F32)
    return spec[:, :width], spec[:, width:]


def medium_blocks(wide, ker_re, ker_im, fore_ref, low_ref, back_ref):
    width = ker_re.shape[1]
    out = []
    for b in range(wide.shape[1] // width - 1):
        window = wide[:, b * width : (b + 2) * width]
        sig = dot(window, fore_ref[...]) + dot(window, low_ref[...])
        sig_re, sig_im = sig[:, :width], sig[:, width:]
        product = jnp.concatenate(
            [
                (sig_re * ker_re - sig_im * ker_im).astype(BF16),
                (sig_re * ker_im + sig_im * ker_re).astype(BF16),
            ],
            axis=1,
        )
        out.append(dot(product, back_ref[...]).astype(BF16))
    return jnp.concatenate(out, axis=1)


def joined(parts, counts):
    refs, out = list(parts), []
    for count in counts:
        total = refs.pop(0)[...].astype(F32)
        for _ in range(count - 1):
            total = total + refs.pop(0)[...].astype(F32)
        out.append(total.astype(BF16))
    return jnp.concatenate(out, axis=1)


def late_kernel(counts, *refs):
    n = sum(counts)
    taps_ref, fore_ref, low_ref, back_ref, oper_ref, edge_ref, out_ref = refs[n:]
    value = joined(refs[:n], counts)
    oper_ref[...] = value
    edge_ref[...] = value[:, -edge_ref.shape[1] :]
    ker_re, ker_im = medium_spectrum(taps_ref[...], fore_ref, low_ref)
    out_ref[...] = medium_blocks(value, ker_re, ker_im, fore_ref, low_ref, back_ref)


def early_kernel(counts, *refs):
    n = sum(counts)
    edge_ref, later_ref, tail_ref, taps_ref, fore_ref, low_ref, back_ref, oper_ref, out_ref = refs[
        n:
    ]
    value = joined(refs[:n], counts)
    later = later_ref[...]
    half = value.shape[1]
    oper_ref[:, :half] = value
    oper_ref[:, half:] = later
    ker_re, ker_im = medium_spectrum(taps_ref[...], fore_ref, low_ref)
    width = ker_re.shape[1]
    wide = jnp.concatenate([edge_ref[...], value, later[:, :width]], axis=1)
    out_ref[:, : half + width] = medium_blocks(wide, ker_re, ker_im, fore_ref, low_ref, back_ref)
    out_ref[:, half + width :] = tail_ref[...]


def medium_call(kernel, parts, extra, taps, tables, widths):
    counts = tuple(len(p) for p in parts)
    arrays = [array for part in parts for array in part] + list(extra)
    channels = arrays[0].shape[0]
    width = taps.shape[0]
    block = min(channels, 256)
    row = lambda n: pl.BlockSpec((block, n), lambda i: (i, 0))
    return pl.pallas_call(
        functools.partial(kernel, counts),
        out_shape=[jax.ShapeDtypeStruct((channels, n), BF16) for n in widths],
        grid=(channels // block,),
        in_specs=[row(array.shape[1]) for array in arrays]
        + [pl.BlockSpec((width, block), lambda i: (0, i))]
        + [whole(t.shape) for t in tables],
        out_specs=[row(n) for n in widths],
        compiler_params=grant(16),
    )(*arrays, taps, *tables)


def ring(block, axis, distance):
    count = lax.axis_size(axis)
    return lax.ppermute(block, axis, [(i, (i + distance) % count) for i in range(count)])


def forward(block, axis):
    count = lax.axis_size(axis)
    return lax.ppermute(block, axis, [(i, i + 1) for i in range(count - 1)])


def swapped(block, axis, bit):
    return lax.ppermute(block, axis, [(i, i ^ bit) for i in range(lax.axis_size(axis))])


def neighbour_weights(ids, out_weight, width):
    slabs = turned(
        ids,
        out_weight,
        width,
        (lambda ids: ids[1] ^ 1 ^ ((ids[0] & 1) * 2), lambda ids: ids[1] ^ 2 ^ (ids[0] & 1)),
    )
    return [swapped(slabs[0], "tp", 1), swapped(slabs[1], "tp", 2)]


def both_cores(sides, after):
    held = lax.optimization_barrier((*sides, after))
    out = []
    for straight in held[:2]:
        out.append((straight, swapped(straight, "ctx", 1)))
    return out, held[2]


def operator_parts(ids, gated, out_weight, weights, sides):
    if sides is None:
        source = jnp.concatenate(gated, axis=1)
        partial = lax.dot_general(
            out_weight, source, (((0,), (0,)), ((), ())), preferred_element_type=F32
        ).astype(BF16)
        return [[lax.psum_scatter(partial, "tp", scatter_dimension=0, tiled=True)]]
    near = [swapped(gated[0], "tp", 1), swapped(gated[1], "tp", 2)]
    send = project(ids, gated, near, (weights[2], weights[1]), sides, 1)
    got = [swapped(send[0], "tp", 2), swapped(send[1], "tp", 1)]
    keep = project(ids, gated, near, (weights[0], weights[0]), sides, 0)
    return [[keep[0], got[0]], [keep[1], got[1]]]


def shards(query_proj, key_proj, value_proj, short_taps, long_filter, out_weight, medium_taps):
    channels, tokens = query_proj.shape
    groups = lax.axis_size("ctx")
    length = long_filter.shape[1]
    tables = long_tables(length, groups)
    ids = jnp.stack([lax.axis_index("ctx"), lax.axis_index("tp")]).astype(jnp.int32)
    tails = [x[:, -2:] for x in (query_proj, key_proj, value_proj)]
    edges = forward(jnp.concatenate(tails, axis=1), "ctx").astype(F32)
    flat_taps = short_taps.reshape(9, channels).T
    aux = jnp.concatenate([flat_taps, edges, jnp.zeros((channels, 1), F32)], axis=1)
    owned = long_filter.shape[0]
    spec = spectra(long_filter, tables, min(owned, 16))
    batch = groups // 2
    far = mix(ids, key_proj, value_proj, aux, batch, batch, groups)
    near = mix(ids, key_proj, value_proj, aux, 0, batch, groups)
    sent = list(near) + list(far)
    sides, weights = None, None
    if lax.axis_size("tp") == 4:
        part = out_weight.shape[1] // 4
        held = lax.optimization_barrier((out_weight, near[0]))
        sent[0] = held[1]
        sides = neighbour_weights(ids, held[0], part)
        weights = turned(
            ids,
            held[0],
            part,
            (lambda ids: ids[1], lambda ids: ids[1] ^ 1, lambda ids: ids[1] ^ 2),
        )
    query = query_conv(query_proj, aux)
    pieces = [sent[0]]
    for s in range(1, groups):
        pieces.append(ring(sent[s], "ctx", s))
    results = list(long_conv(ids, pieces, spec, tables, min(owned, 32)))
    if sides is not None:
        sides, results[0] = both_cores(sides, results[0])
    width = medium_taps.shape[0]
    half = tokens // 2
    done = []
    for h in (1, 0):
        mine = results[h::2]
        back = [mine[0]] + [ring(mine[s], "ctx", s) for s in range(1, groups)]
        gated = gate(ids, back, query, h * half // LANES)
        parts = operator_parts(ids, gated, out_weight, weights, sides)
        if h == 1:
            later, edge, tail = medium_call(
                late_kernel,
                parts,
                (),
                medium_taps,
                medium_tables(width),
                (half, width, half - width),
            )
            edge = forward(edge, "ctx")
        else:
            done = medium_call(
                early_kernel,
                parts,
                (edge, later, tail),
                medium_taps,
                medium_tables(width),
                (tokens, tokens),
            )
    return tuple(done)


def solution(mesh):
    in_specs = (
        P("tp", "ctx"),
        P("tp", "ctx"),
        P("tp", "ctx"),
        P(None, None, "tp"),
        P(("tp", "ctx"), None),
        P("tp", None),
        P(None, "tp"),
    )
    out_specs = (P("tp", "ctx"), P("tp", "ctx"))
    return jax.shard_map(shards, mesh=mesh, in_specs=in_specs, out_specs=out_specs, check_vma=False)
```

```python
import functools
import math

import jax
import jax.numpy as jnp
import numpy as np
from jax import lax
from jax.experimental import pallas as pl
from jax.experimental.pallas import tpu as pltpu
from jax.sharding import PartitionSpec as P


LANES = 128
BF16 = jnp.bfloat16
F32 = jnp.float32


def split_table(table):
    high = np.asarray(table, np.float32).astype(BF16)
    low = (np.asarray(table, np.float64) - high.astype(np.float64)).astype(BF16)
    return high, low


def rotation(rows, cols, period):
    angles = 2.0 * math.pi * np.outer(rows, cols) / period
    return np.cos(angles), np.sin(angles)


@functools.lru_cache
def long_tables(length, groups):
    n1 = length // LANES
    first = np.arange(n1)
    lanes = np.arange(LANES)
    cos1, sin1 = rotation(first + 0.25, first, n1)
    outer = np.concatenate([cos1, -sin1], axis=0)
    back = np.concatenate([cos1.T, -sin1.T], axis=1) / n1
    twist_re, twist_im = rotation(first + 0.25, lanes, length)
    cos2, sin2 = rotation(lanes, lanes, LANES)
    inner = np.block([[cos2, -sin2], [sin2, cos2]])
    inner_back = np.block([[cos2, sin2], [-sin2, cos2]]) / LANES
    per = n1 // groups
    fore, rear = [], []
    for me in range(groups):
        ids, out = (me - np.arange(groups)) % groups, (me + np.arange(groups)) % groups
        ids = (ids[:, None] * per + np.arange(per)).reshape(-1)
        out = (out[:, None] * per + np.arange(per)).reshape(-1)
        high, low = split_table(outer[:, ids])
        fore.append(np.concatenate([high, low], axis=1))
        high, low = split_table(back[out])
        rear.append(np.concatenate([high, low], axis=1))
    high, low = split_table(outer)
    plain = np.concatenate([high, high, low], axis=1)
    twist = np.stack([twist_re, -twist_im]).astype(np.float32)
    inner_high, inner_low = split_table(inner)
    return dict(
        fore=np.stack(fore),
        rear=np.stack(rear),
        plain=plain,
        twist=twist,
        inner=inner_high,
        inner_low=inner_low,
        inner_back=split_table(inner_back)[0],
    )


@functools.lru_cache
def medium_tables(width):
    span = 2 * width
    cos, sin = rotation(np.arange(span), np.arange(width) + 0.5, span)
    high, low = split_table(np.concatenate([cos, -sin], axis=1))
    last = slice(width, span)
    back = np.concatenate([cos[last].T, -sin[last].T], axis=0) / width
    return high, low, split_table(back)[0]


def grant(mib):
    return pltpu.CompilerParams(vmem_limit_bytes=mib * 1024 * 1024)


def dot(left, right):
    return jnp.dot(left, right, preferred_element_type=F32)


def short_conv(block, edge, taps):
    lane = lax.broadcasted_iota(jnp.int32, block.shape, 1)
    older, newer = edge[:, 0:1], edge[:, 1:2]
    back1 = jnp.where(lane == 0, newer, pltpu.roll(block, 1, 1))
    back2 = jnp.where(lane == 0, older, jnp.where(lane == 1, newer, pltpu.roll(block, 2, 1)))
    return taps[:, 0:1] * block + taps[:, 1:2] * back1 + taps[:, 2:3] * back2


def mix_kernel(ids_ref, key_ref, value_ref, aux_ref, *out_refs):
    aux = aux_ref[...]
    keys = short_conv(key_ref[...].astype(F32), aux[:, 11:13], aux[:, 3:6])
    values = short_conv(value_ref[...].astype(F32), aux[:, 13:15], aux[:, 6:9])
    mixed = (keys * values).astype(BF16)

    for at, out_ref in enumerate(out_refs):

        @pl.when(pl.program_id(0) == at)
        def _():
            for j in range(out_ref.shape[0]):
                out_ref[j] = mixed[:, j * LANES : (j + 1) * LANES]


def mix(ids, key_proj, value_proj, aux, groups, chunk, chunks):
    channels, tokens = key_proj.shape
    rows = channels // groups // chunks
    count = tokens // LANES

    where = lambda g, ids: (lax.rem(ids[0] + g, groups) * chunks + chunk, 0)
    return pl.pallas_call(
        mix_kernel,
        out_shape=[jax.ShapeDtypeStruct((count, rows, LANES), BF16)] * groups,
        grid_spec=pltpu.PrefetchScalarGridSpec(
            num_scalar_prefetch=1,
            grid=(groups,),
            in_specs=[
                pl.BlockSpec((rows, tokens), where),
                pl.BlockSpec((rows, tokens), where),
                pl.BlockSpec((rows, aux.shape[1]), where),
            ],
            out_specs=[whole((count, rows, LANES))] * groups,
        ),
        compiler_params=grant(6),
        name="mix",
    )(ids, key_proj, value_proj, aux)


def twisted(wide, twist_re, twist_im, count):
    half = wide.shape[0] // 2
    out = []
    for c in range(count):
        re = wide[:half, c * LANES : (c + 1) * LANES]
        im = wide[half:, c * LANES : (c + 1) * LANES]
        out.append((re * twist_re - im * twist_im, re * twist_im + im * twist_re))
    return out


def filter_kernel(filter_ref, plain_ref, twist_ref, inner_ref, inner_low_ref, out_ref, rows_ref):
    block = filter_ref.shape[0]
    n1 = filter_ref.shape[1] // LANES
    for n in range(n1):
        rows_ref[n * block : (n + 1) * block, :] = filter_ref[:, n * LANES : (n + 1) * LANES]

    group = math.gcd(block, 8)

    def body(at, carry):
        base = at * group
        highs, lows = [], []
        for pair in range(group // 2):
            loaded = [
                rows_ref[pl.ds(base + 2 * pair + c, n1, stride=block), :] for c in range(2)
            ]
            both = jnp.concatenate(loaded, axis=1)
            high = both.astype(BF16)
            low = (both - high.astype(F32)).astype(BF16)
            wide = dot(plain_ref[...], jnp.concatenate([high, low, high], axis=0))
            for re, im in twisted(wide, twist_ref[0], twist_ref[1], 2):
                line = jnp.concatenate([re, im], axis=1)
                high = line.astype(BF16)
                highs.append(high)
                lows.append((line - high.astype(F32)).astype(BF16))
        high = jnp.concatenate(highs, axis=0)
        low = jnp.concatenate(lows, axis=0)
        spectrum = (
            dot(high, inner_ref[...]) + dot(low, inner_ref[...]) + dot(high, inner_low_ref[...])
        )
        out_ref[pl.ds(base, group)] = spectrum.reshape(group, n1, 2 * LANES)
        return carry

    lax.fori_loop(0, block // group, body, 0)


def whole(shape):
    return pl.BlockSpec(shape, lambda *_: (0,) * len(shape))


def spectra(long_filter, tables, block):
    channels, length = long_filter.shape
    n1 = length // LANES
    names = ("plain", "twist", "inner", "inner_low")
    return pl.pallas_call(
        filter_kernel,
        out_shape=jax.ShapeDtypeStruct((channels, n1, 2 * LANES), F32),
        grid=(channels // block,),
        in_specs=[pl.BlockSpec((block, length), lambda i: (i, 0))]
        + [whole(tables[name].shape) for name in names],
        out_specs=pl.BlockSpec((block, n1, 2 * LANES), lambda i: (i, 0, 0)),
        scratch_shapes=[pltpu.VMEM((n1 * block, LANES), F32)],
        compiler_params=grant(9),
        name="spectra",
    )(long_filter, *[tables[name] for name in names])


def conv_kernel(count, ids_ref, *refs):
    pieces = refs[:count]
    spec_ref, fore_ref, rear_ref, twist_ref, inner_ref, back_ref = refs[count : count + 6]
    outs, (rows_ref, done_ref) = refs[count + 6 : -2], refs[-2:]
    per, block, _ = pieces[0].shape
    at = 0
    for piece_ref in pieces:
        size = per * block
        rows_ref[at : at + size, :] = piece_ref[...].astype(F32).reshape(size, LANES)
        at += size
    n1 = at // block
    group = math.gcd(block, 8)

    def body(at, carry):
        base = at * group
        lines = []
        for pair in range(group // 2):
            loaded = [
                rows_ref[pl.ds(base + 2 * pair + c, n1, stride=block), :].astype(BF16)
                for c in range(2)
            ]
            both = jnp.concatenate(loaded, axis=1)
            wide = dot(fore_ref[0], jnp.concatenate([both, both], axis=0))
            for re, im in twisted(wide, twist_ref[0], twist_ref[1], 2):
                lines.append(jnp.concatenate([re.astype(BF16), im.astype(BF16)], axis=1))
        spectrum = dot(jnp.concatenate(lines, axis=0), inner_ref[...])
        other = spec_ref[pl.ds(base, group)].reshape(group * n1, 2 * LANES)
        sig_re, sig_im = spectrum[:, :LANES], spectrum[:, LANES:]
        ker_re, ker_im = other[:, :LANES], other[:, LANES:]
        product = jnp.concatenate(
            [
                (sig_re * ker_re - sig_im * ker_im).astype(BF16),
                (sig_re * ker_im + sig_im * ker_re).astype(BF16),
            ],
            axis=1,
        )
        turned = dot(product, back_ref[...])
        for pair in range(group // 2):
            stacks = []
            for c in range(2):
                at_row = (2 * pair + c) * n1
                re = turned[at_row : at_row + n1, :LANES]
                im = turned[at_row : at_row + n1, LANES:]
                top = (re * twist_ref[0] + im * twist_ref[1]).astype(BF16)
                low = (im * twist_ref[0] - re * twist_ref[1]).astype(BF16)
                stacks.append(jnp.concatenate([top, low, top, low], axis=0))
            result = dot(rear_ref[0], jnp.concatenate(stacks, axis=1))
            for c in range(2):
                done_ref[pl.ds(base + 2 * pair + c, n1, stride=block), :] = result[
                    :, c * LANES : (c + 1) * LANES
                ]
        return carry

    lax.fori_loop(0, block // group, body, 0)
    at = 0
    for out_ref in outs:
        size = math.prod(out_ref.shape[:-1])
        out_ref[...] = done_ref[at : at + size, :].reshape(out_ref.shape).astype(BF16)
        at += size


def long_conv(ids, pieces, spec, tables, block, tiles, first):
    groups = len(pieces)
    per, channels, _ = pieces[0].shape
    n1 = groups * per
    runs = list(tiles) * groups
    tile = lambda n: pl.BlockSpec((n, block, LANES), lambda i, ids: (0, i, 0))
    mine = lambda shape: pl.BlockSpec((1,) + shape[1:], lambda i, ids: (ids[0], 0, 0))
    names = ("fore", "rear", "twist", "inner", "inner_back")
    return pl.pallas_call(
        functools.partial(conv_kernel, groups),
        out_shape=[jax.ShapeDtypeStruct((n, channels, LANES), BF16) for n in runs],
        grid_spec=pltpu.PrefetchScalarGridSpec(
            num_scalar_prefetch=1,
            grid=(channels // block,),
            in_specs=[tile(per)] * groups
            + [pl.BlockSpec((block, n1, 2 * LANES), lambda i, ids: (i + first // block, 0, 0))]
            + [mine(tables[name].shape) for name in names[:2]]
            + [whole(tables[name].shape) for name in names[2:]],
            out_specs=[tile(n) for n in runs],
            scratch_shapes=[pltpu.VMEM((n1 * block, LANES), F32)] * 2,
        ),
        compiler_params=grant(14),
        name="conv",
    )(ids, *pieces, spec, *[tables[name] for name in names])


def query_kernel(query_ref, aux_ref, out_ref):
    aux = aux_ref[...]
    query = short_conv(query_ref[...].astype(F32), aux[:, 9:11], aux[:, 0:3])
    for j in range(out_ref.shape[0]):
        out_ref[j] = query[:, j * LANES : (j + 1) * LANES]


def query_conv(query_proj, aux):
    channels, tokens = query_proj.shape
    block = min(channels, 128)
    count = tokens // LANES
    return pl.pallas_call(
        query_kernel,
        out_shape=jax.ShapeDtypeStruct((count, channels, LANES), F32),
        grid=(channels // block,),
        in_specs=[
            pl.BlockSpec((block, tokens), lambda i: (i, 0)),
            pl.BlockSpec((block, aux.shape[1]), lambda i: (i, 0)),
        ],
        out_specs=pl.BlockSpec((count, block, LANES), lambda i: (0, i, 0)),
        compiler_params=grant(4),
        name="query",
    )(query_proj, aux)


def gate_kernel(chunk, chunks, tiles, ids_ref, *refs):
    pieces, (query_ref, left_ref, right_ref) = refs[:-3], refs[-3:]
    groups = len(pieces)
    rows = pieces[0].shape[1]
    for side, out_ref in enumerate((left_ref, right_ref)):

        @pl.when(lax.rem(pl.program_id(0), tiles) // (tiles // 2) == side)
        def _():
            for s, piece_ref in enumerate(pieces):
                group = lax.rem(ids_ref[0] + groups - s, groups)
                at = pl.ds(pl.multiple_of((group * chunks + chunk) * rows, rows), rows)
                to = pl.ds(pl.multiple_of(group * rows, rows), rows)
                conv = piece_ref[0].astype(F32)
                out_ref[to, :] = (query_ref[0, at, :] * conv).astype(BF16)


def gate(ids, pieces, query, chunk, chunks, start, tiles):
    groups = len(pieces)
    per, rows, _ = pieces[0].shape
    channels = query.shape[1]
    half = tiles // 2
    shape = (groups * rows, per // 2 * LANES)
    block = (groups * rows, LANES)
    left = lambda j, ids: (0, j // tiles * half + jnp.minimum(lax.rem(j, tiles), half - 1))
    right = lambda j, ids: (0, j // tiles * half + jnp.maximum(lax.rem(j, tiles) - half, 0))
    return pl.pallas_call(
        functools.partial(gate_kernel, chunk, chunks, tiles),
        out_shape=[jax.ShapeDtypeStruct(shape, BF16)] * 2,
        grid_spec=pltpu.PrefetchScalarGridSpec(
            num_scalar_prefetch=1,
            grid=(per,),
            in_specs=[pl.BlockSpec((1, rows, LANES), lambda j, ids: (j, 0, 0))] * groups
            + [pl.BlockSpec((1, channels, LANES), lambda j, ids: (start + j, 0, 0))],
            out_specs=[pl.BlockSpec(block, left), pl.BlockSpec(block, right)],
        ),
        compiler_params=grant(5),
        name="gate",
    )(ids, *pieces, query)


def turn_kernel(groups, chunks, ids_ref, weight_ref, *out_refs):
    rows = weight_ref.shape[0] // groups // chunks
    for at, out_ref in enumerate(out_refs):

        @pl.when(pl.program_id(0) == at)
        def _():
            parts = [
                weight_ref[(g * chunks + c) * rows : (g * chunks + c + 1) * rows, :]
                for c in range(chunks)
                for g in range(groups)
            ]
            out_ref[...] = jnp.concatenate(parts, axis=0).T


def turned(ids, out_weight, width, shards_of, groups, chunks):
    channels = out_weight.shape[0]
    step = min(width, 256)
    inner = width // step
    count = len(shards_of)

    def from_at(k, h, ids):
        shard = shards_of[0](ids)
        for at in range(1, count):
            shard = jnp.where(k == at, shards_of[at](ids), shard)
        return (0, shard * inner + h)

    def out_at(mine):
        return lambda k, h, ids: (
            jnp.where(k == mine, h, jnp.where(k < mine, 0, inner - 1)),
            0,
        )

    return pl.pallas_call(
        functools.partial(turn_kernel, groups, chunks),
        out_shape=[jax.ShapeDtypeStruct((width, channels), BF16)] * count,
        grid_spec=pltpu.PrefetchScalarGridSpec(
            num_scalar_prefetch=1,
            grid=(count, inner),
            in_specs=[pl.BlockSpec((channels, step), from_at)],
            out_specs=[pl.BlockSpec((step, channels), out_at(at)) for at in range(count)],
        ),
        compiler_params=grant(7),
        name="turn",
    )(ids, out_weight)


def project_kernel(slot, chunks, ids_ref, *refs):
    sources, refs = refs[: 4 * chunks], refs[4 * chunks :]
    weights, sides, outs = refs[0:2], (refs[2:4], refs[4:6]), refs[6:8]
    for colour in range(2):
        for partner in range(2):

            @pl.when((pl.program_id(0) == colour) & (((ids_ref[0] & 1) ^ slot) == partner))
            def _():
                total = None
                for near, table in enumerate((weights[colour], sides[colour][partner])):
                    stack = [sources[(2 * c + near) * 2 + colour][...] for c in range(chunks)]
                    term = dot(table[...], jnp.concatenate(stack, axis=0))
                    total = term if total is None else total + term
                outs[colour][...] = total.astype(BF16)


def project(ids, sources, weights, sides, slot, h):
    width, channels = weights[0].shape
    flat = [array for own, near in sources for array in (*own, *near)]
    tokens = min(array.shape[1] for array in flat)
    step = min(width, 512)
    inner = width // step

    def source(array):
        at = h if array.shape[1] > tokens else 0
        return pl.BlockSpec((array.shape[0], tokens), lambda *_: (0, at))

    def when(active, mine, colour, h):
        return (jnp.where(active, h, jnp.where(colour > mine, inner - 1, 0)), 0)

    def side_at(mine, partner):
        def at(colour, h, ids):
            chosen = ((ids[0] & 1) ^ slot) == partner
            return when((colour == mine) & chosen, mine, jnp.where(chosen, colour, mine), h)

        return at

    def colour_at(mine):
        return lambda colour, h, ids: when(colour == mine, mine, colour, h)

    return pl.pallas_call(
        functools.partial(project_kernel, slot, len(sources)),
        out_shape=[jax.ShapeDtypeStruct((width, tokens), BF16)] * 2,
        grid_spec=pltpu.PrefetchScalarGridSpec(
            num_scalar_prefetch=1,
            grid=(2, inner),
            in_specs=[source(array) for array in flat]
            + [pl.BlockSpec((step, channels), colour_at(colour)) for colour in range(2)]
            + [
                pl.BlockSpec((step, channels), side_at(colour, partner))
                for colour in range(2)
                for partner in range(2)
            ],
            out_specs=[pl.BlockSpec((step, tokens), colour_at(colour)) for colour in range(2)],
        ),
        compiler_params=grant(18),
        name="project",
    )(ids, *flat, *weights, *sides[0], *sides[1])


def medium_spectrum(taps, fore_ref, low_ref):
    width = taps.shape[0]
    over_taps = (((0,), (0,)), ((), ()))
    spec = lax.dot_general(taps, fore_ref[:width], over_taps, preferred_element_type=F32)
    spec = spec + lax.dot_general(taps, low_ref[:width], over_taps, preferred_element_type=F32)
    return spec[:, :width], spec[:, width:]


def medium_blocks(wide, ker_re, ker_im, fore_ref, low_ref, back_ref):
    width = ker_re.shape[1]
    out = []
    for b in range(wide.shape[1] // width - 1):
        window = wide[:, b * width : (b + 2) * width]
        sig = dot(window, fore_ref[...]) + dot(window, low_ref[...])
        sig_re, sig_im = sig[:, :width], sig[:, width:]
        product = jnp.concatenate(
            [
                (sig_re * ker_re - sig_im * ker_im).astype(BF16),
                (sig_re * ker_im + sig_im * ker_re).astype(BF16),
            ],
            axis=1,
        )
        out.append(dot(product, back_ref[...]).astype(BF16))
    return jnp.concatenate(out, axis=1)


def joined(parts, counts):
    refs, out = list(parts), []
    for count in counts:
        total = refs.pop(0)[...].astype(F32)
        for _ in range(count - 1):
            total = total + refs.pop(0)[...].astype(F32)
        out.append(total.astype(BF16))
    return jnp.concatenate(out, axis=1)


def late_kernel(counts, *refs):
    n = sum(counts)
    taps_ref, fore_ref, low_ref, back_ref, oper_ref, edge_ref, out_ref = refs[n:]
    value = joined(refs[:n], counts)
    oper_ref[...] = value
    edge_ref[...] = value[:, -edge_ref.shape[1] :]
    ker_re, ker_im = medium_spectrum(taps_ref[...], fore_ref, low_ref)
    out_ref[...] = medium_blocks(value, ker_re, ker_im, fore_ref, low_ref, back_ref)


def early_kernel(counts, *refs):
    n = sum(counts)
    edge_ref, later_ref, tail_ref, taps_ref, fore_ref, low_ref, back_ref, oper_ref, out_ref = refs[
        n:
    ]
    value = joined(refs[:n], counts)
    later = later_ref[...]
    half = value.shape[1]
    oper_ref[:, :half] = value
    oper_ref[:, half:] = later
    ker_re, ker_im = medium_spectrum(taps_ref[...], fore_ref, low_ref)
    width = ker_re.shape[1]
    wide = jnp.concatenate([edge_ref[...], value, later[:, :width]], axis=1)
    out_ref[:, : half + width] = medium_blocks(wide, ker_re, ker_im, fore_ref, low_ref, back_ref)
    out_ref[:, half + width :] = tail_ref[...]


def medium_call(kernel, parts, extra, taps, tables, widths):
    counts = tuple(len(p) for p in parts)
    arrays = [array for part in parts for array in part] + list(extra)
    channels = arrays[0].shape[0]
    width = taps.shape[0]
    block = min(channels, 256)
    row = lambda n: pl.BlockSpec((block, n), lambda i: (i, 0))
    return pl.pallas_call(
        functools.partial(kernel, counts),
        out_shape=[jax.ShapeDtypeStruct((channels, n), BF16) for n in widths],
        grid=(channels // block,),
        in_specs=[row(array.shape[1]) for array in arrays]
        + [pl.BlockSpec((width, block), lambda i: (0, i))]
        + [whole(t.shape) for t in tables],
        out_specs=[row(n) for n in widths],
        compiler_params=grant(10),
    )(*arrays, taps, *tables)


def ring(block, axis, distance):
    count = lax.axis_size(axis)
    if distance == 0:
        return block
    return lax.ppermute(block, axis, [(i, (i + distance) % count) for i in range(count)])


def forward(block, axis):
    count = lax.axis_size(axis)
    return lax.ppermute(block, axis, [(i, i + 1) for i in range(count - 1)])


def swapped(block, axis, bit):
    return lax.ppermute(block, axis, [(i, i ^ bit) for i in range(lax.axis_size(axis))])


def neighbour_weights(ids, out_weight, width, groups, chunks):
    slabs = turned(
        ids,
        out_weight,
        width,
        (lambda ids: ids[1] ^ 1 ^ ((ids[0] & 1) * 2), lambda ids: ids[1] ^ 2 ^ (ids[0] & 1)),
        groups,
        chunks,
    )
    return [swapped(slabs[0], "tp", 1), swapped(slabs[1], "tp", 2)]


def both_cores(sides, after):
    held = lax.optimization_barrier((*sides, after))
    out = []
    for straight in held[:2]:
        out.append((straight, swapped(straight, "ctx", 1)))
    return out, held[2]


def neighbours(gated):
    return [swapped(gated[0], "tp", 1), swapped(gated[1], "tp", 2)]


def shards(query_proj, key_proj, value_proj, short_taps, long_filter, out_weight, medium_taps):
    channels, tokens = query_proj.shape
    groups = lax.axis_size("ctx")
    length = long_filter.shape[1]
    tables = long_tables(length, groups)
    ids = jnp.stack([lax.axis_index("ctx"), lax.axis_index("tp")]).astype(jnp.int32)
    tails = [x[:, -2:] for x in (query_proj, key_proj, value_proj)]
    edges = forward(jnp.concatenate(tails, axis=1), "ctx").astype(F32)
    flat_taps = short_taps.reshape(9, channels).T
    aux = jnp.concatenate([flat_taps, edges, jnp.zeros((channels, 1), F32)], axis=1)
    owned = long_filter.shape[0]
    four = lax.axis_size("tp") == 4
    chunks = 2 if four and owned % 32 == 0 else 1
    rows = owned // chunks
    spec = spectra(long_filter, tables, min(owned, 16))
    sent = []
    for c in range(chunks):
        sent.append(list(mix(ids, key_proj, value_proj, aux, groups, c, chunks)))
    sides, weights = None, None
    if four:
        part = out_weight.shape[1] // 4
        held = lax.optimization_barrier((out_weight, sent[-1][0]))
        sent[-1][0] = held[1]
        sides = neighbour_weights(ids, held[0], part, groups, chunks)
        weights = turned(
            ids,
            held[0],
            part,
            (lambda ids: ids[1], lambda ids: ids[1] ^ 1, lambda ids: ids[1] ^ 2),
            groups,
            chunks,
        )
    query = query_conv(query_proj, aux)
    count = tokens // LANES
    half_tiles = count // 2
    own = {0: [], 1: []}
    near = {0: [], 1: []}
    for c in range(chunks):
        last = c == chunks - 1
        got = [ring(piece, "ctx", s) for s, piece in enumerate(sent[c])]
        runs = (half_tiles, half_tiles) if last else (count,)
        results = list(long_conv(ids, got, spec, tables, min(rows, 32), runs, c * rows))
        for h in (1, 0) if last else (None,):
            back = [
                ring(piece, "ctx", s)
                for s, piece in enumerate(results[h::2] if last else results)
            ]
            start = h * half_tiles if last else 0
            gated = list(gate(ids, back, query, c, chunks, start, half_tiles))
            if four and c == 0 and h != 0:
                sides, gated[0] = both_cores(sides, gated[0])
            beside = neighbours(gated) if four else None
            for at in (h,) if last else (0, 1):
                own[at].append(gated)
                near[at].append(beside)
    parts = {}
    for h in (1, 0):
        if not four:
            source = jnp.concatenate(own[h][0], axis=1)
            partial = lax.dot_general(
                out_weight, source, (((0,), (0,)), ((), ())), preferred_element_type=F32
            ).astype(BF16)
            parts[h] = [[lax.psum_scatter(partial, "tp", scatter_dimension=0, tiled=True)]]
            continue
        sources = list(zip(own[h], near[h]))
        send = project(ids, sources, (weights[2], weights[1]), sides, 1, h)
        got = [swapped(send[0], "tp", 2), swapped(send[1], "tp", 1)]
        keep = project(ids, sources, (weights[0], weights[0]), sides, 0, h)
        parts[h] = [[keep[0], got[0]], [keep[1], got[1]]]
    width = medium_taps.shape[0]
    half = tokens // 2
    tables = medium_tables(width)
    later, edge, tail = medium_call(
        late_kernel, parts[1], (), medium_taps, tables, (half, width, half - width)
    )
    edge = forward(edge, "ctx")
    return tuple(
        medium_call(
            early_kernel, parts[0], (edge, later, tail), medium_taps, tables, (tokens, tokens)
        )
    )


def solution(mesh):
    in_specs = (
        P("tp", "ctx"),
        P("tp", "ctx"),
        P("tp", "ctx"),
        P(None, None, "tp"),
        P(("tp", "ctx"), None),
        P("tp", None),
        P(None, "tp"),
    )
    out_specs = (P("tp", "ctx"), P("tp", "ctx"))
    return jax.shard_map(shards, mesh=mesh, in_specs=in_specs, out_specs=out_specs, check_vma=False)
```

```python
import functools
import math

import jax
import jax.numpy as jnp
import numpy as np
from jax import lax
from jax.experimental import pallas as pl
from jax.experimental.pallas import tpu as pltpu
from jax.sharding import PartitionSpec as P


LANES = 128
BF16 = jnp.bfloat16
F32 = jnp.float32


def split_table(table):
    high = np.asarray(table, np.float32).astype(BF16)
    low = (np.asarray(table, np.float64) - high.astype(np.float64)).astype(BF16)
    return high, low


def rotation(rows, cols, period):
    angles = 2.0 * math.pi * np.outer(rows, cols) / period
    return np.cos(angles), np.sin(angles)


@functools.lru_cache
def long_tables(length, groups):
    n1 = length // LANES
    first = np.arange(n1)
    lanes = np.arange(LANES)
    cos1, sin1 = rotation(first + 0.25, first, n1)
    outer = np.concatenate([cos1, -sin1], axis=0)
    back = np.concatenate([cos1.T, -sin1.T], axis=1) / n1
    twist_re, twist_im = rotation(first + 0.25, lanes, length)
    cos2, sin2 = rotation(lanes, lanes, LANES)
    inner = np.block([[cos2, -sin2], [sin2, cos2]])
    inner_back = np.block([[cos2, sin2], [-sin2, cos2]]) / LANES
    per = n1 // groups
    fore, rear = [], []
    for me in range(groups):
        ids, out = (me - np.arange(groups)) % groups, (me + np.arange(groups)) % groups
        ids = (ids[:, None] * per + np.arange(per)).reshape(-1)
        out = (out[:, None] * per + np.arange(per)).reshape(-1)
        high, low = split_table(outer[:, ids])
        fore.append(np.concatenate([high, low], axis=1))
        high, low = split_table(back[out])
        rear.append(np.concatenate([high, low], axis=1))
    high, low = split_table(outer)
    plain = np.concatenate([high, high, low], axis=1)
    twist = np.stack([twist_re, -twist_im]).astype(np.float32)
    inner_high = split_table(inner)[0]
    return dict(
        fore=np.stack(fore),
        rear=np.stack(rear),
        plain=plain,
        twist=twist,
        inner=inner_high,
        inner_back=split_table(inner_back)[0],
    )


@functools.lru_cache
def medium_tables(width):
    span = 2 * width
    cos, sin = rotation(np.arange(span), np.arange(width) + 0.5, span)
    fore = split_table(np.concatenate([cos, -sin], axis=1))[0]
    last = slice(width, span)
    back = np.concatenate([cos[last].T, -sin[last].T], axis=0) / width
    return fore, split_table(back)[0]


def grant(mib):
    return pltpu.CompilerParams(vmem_limit_bytes=mib * 1024 * 1024)


def dot(left, right):
    return jnp.dot(left, right, preferred_element_type=F32)


def short_conv(block, edge, taps):
    lane = lax.broadcasted_iota(jnp.int32, block.shape, 1)
    older, newer = edge[:, 0:1], edge[:, 1:2]
    back1 = jnp.where(lane == 0, newer, pltpu.roll(block, 1, 1))
    back2 = jnp.where(lane == 0, older, jnp.where(lane == 1, newer, pltpu.roll(block, 2, 1)))
    return taps[:, 0:1] * block + taps[:, 1:2] * back1 + taps[:, 2:3] * back2


def mix_kernel(ids_ref, key_ref, value_ref, aux_ref, *out_refs):
    aux = aux_ref[...]
    keys = short_conv(key_ref[...].astype(F32), aux[:, 11:13], aux[:, 3:6])
    values = short_conv(value_ref[...].astype(F32), aux[:, 13:15], aux[:, 6:9])
    mixed = (keys * values).astype(BF16)

    for at, out_ref in enumerate(out_refs):

        @pl.when(pl.program_id(0) == at)
        def _():
            for j in range(out_ref.shape[0]):
                out_ref[j] = mixed[:, j * LANES : (j + 1) * LANES]


def mix(ids, key_proj, value_proj, aux, groups, chunk, chunks):
    channels, tokens = key_proj.shape
    rows = channels // groups // chunks
    count = tokens // LANES

    where = lambda g, ids: (lax.rem(ids[0] + g, groups) * chunks + chunk, 0)
    return pl.pallas_call(
        mix_kernel,
        out_shape=[jax.ShapeDtypeStruct((count, rows, LANES), BF16)] * groups,
        grid_spec=pltpu.PrefetchScalarGridSpec(
            num_scalar_prefetch=1,
            grid=(groups,),
            in_specs=[
                pl.BlockSpec((rows, tokens), where),
                pl.BlockSpec((rows, tokens), where),
                pl.BlockSpec((rows, aux.shape[1]), where),
            ],
            out_specs=[whole((count, rows, LANES))] * groups,
        ),
        compiler_params=grant(6),
        name="mix",
    )(ids, key_proj, value_proj, aux)


def twisted(wide, twist_re, twist_im, count):
    half = wide.shape[0] // 2
    out = []
    for c in range(count):
        re = wide[:half, c * LANES : (c + 1) * LANES]
        im = wide[half:, c * LANES : (c + 1) * LANES]
        out.append((re * twist_re - im * twist_im, re * twist_im + im * twist_re))
    return out


def filter_kernel(filter_ref, plain_ref, twist_ref, inner_ref, out_ref, rows_ref):
    block = filter_ref.shape[0]
    n1 = filter_ref.shape[1] // LANES
    for n in range(n1):
        rows_ref[n * block : (n + 1) * block, :] = filter_ref[:, n * LANES : (n + 1) * LANES]

    group = math.gcd(block, 8)

    def body(at, carry):
        base = at * group
        lines = []
        for pair in range(group // 2):
            loaded = [
                rows_ref[pl.ds(base + 2 * pair + c, n1, stride=block), :] for c in range(2)
            ]
            both = jnp.concatenate(loaded, axis=1)
            high = both.astype(BF16)
            low = (both - high.astype(F32)).astype(BF16)
            wide = dot(plain_ref[...], jnp.concatenate([high, low, high], axis=0))
            for re, im in twisted(wide, twist_ref[0], twist_ref[1], 2):
                lines.append(jnp.concatenate([re.astype(BF16), im.astype(BF16)], axis=1))
        spectrum = dot(jnp.concatenate(lines, axis=0), inner_ref[...])
        out_ref[pl.ds(base, group)] = spectrum.reshape(group, n1, 2 * LANES)
        return carry

    lax.fori_loop(0, block // group, body, 0)


def whole(shape):
    return pl.BlockSpec(shape, lambda *_: (0,) * len(shape))


def spectra(long_filter, tables, block):
    channels, length = long_filter.shape
    n1 = length // LANES
    names = ("plain", "twist", "inner")
    return pl.pallas_call(
        filter_kernel,
        out_shape=jax.ShapeDtypeStruct((channels, n1, 2 * LANES), F32),
        grid=(channels // block,),
        in_specs=[pl.BlockSpec((block, length), lambda i: (i, 0))]
        + [whole(tables[name].shape) for name in names],
        out_specs=pl.BlockSpec((block, n1, 2 * LANES), lambda i: (i, 0, 0)),
        scratch_shapes=[pltpu.VMEM((n1 * block, LANES), F32)],
        compiler_params=grant(9),
        name="spectra",
    )(long_filter, *[tables[name] for name in names])


def conv_kernel(count, ids_ref, *refs):
    pieces = refs[:count]
    spec_ref, fore_ref, rear_ref, twist_ref, inner_ref, back_ref = refs[count : count + 6]
    outs, (rows_ref, done_ref) = refs[count + 6 : -2], refs[-2:]
    per, block, _ = pieces[0].shape
    at = 0
    for piece_ref in pieces:
        size = per * block
        rows_ref[at : at + size, :] = piece_ref[...].astype(F32).reshape(size, LANES)
        at += size
    n1 = at // block
    group = math.gcd(block, 8)

    def body(at, carry):
        base = at * group
        lines = []
        for pair in range(group // 2):
            loaded = [
                rows_ref[pl.ds(base + 2 * pair + c, n1, stride=block), :].astype(BF16)
                for c in range(2)
            ]
            both = jnp.concatenate(loaded, axis=1)
            wide = dot(fore_ref[0], jnp.concatenate([both, both], axis=0))
            for re, im in twisted(wide, twist_ref[0], twist_ref[1], 2):
                lines.append(jnp.concatenate([re.astype(BF16), im.astype(BF16)], axis=1))
        spectrum = dot(jnp.concatenate(lines, axis=0), inner_ref[...])
        other = spec_ref[pl.ds(base, group)].reshape(group * n1, 2 * LANES)
        sig_re, sig_im = spectrum[:, :LANES], spectrum[:, LANES:]
        ker_re, ker_im = other[:, :LANES], other[:, LANES:]
        product = jnp.concatenate(
            [
                (sig_re * ker_re - sig_im * ker_im).astype(BF16),
                (sig_re * ker_im + sig_im * ker_re).astype(BF16),
            ],
            axis=1,
        )
        turned = dot(product, back_ref[...])
        for pair in range(group // 2):
            stacks = []
            for c in range(2):
                at_row = (2 * pair + c) * n1
                re = turned[at_row : at_row + n1, :LANES]
                im = turned[at_row : at_row + n1, LANES:]
                top = (re * twist_ref[0] + im * twist_ref[1]).astype(BF16)
                low = (im * twist_ref[0] - re * twist_ref[1]).astype(BF16)
                stacks.append(jnp.concatenate([top, low, top, low], axis=0))
            result = dot(rear_ref[0], jnp.concatenate(stacks, axis=1))
            for c in range(2):
                done_ref[pl.ds(base + 2 * pair + c, n1, stride=block), :] = result[
                    :, c * LANES : (c + 1) * LANES
                ]
        return carry

    lax.fori_loop(0, block // group, body, 0)
    at = 0
    for out_ref in outs:
        size = math.prod(out_ref.shape[:-1])
        out_ref[...] = done_ref[at : at + size, :].reshape(out_ref.shape).astype(BF16)
        at += size


def long_conv(ids, pieces, spec, tables, block, tiles, first):
    groups = len(pieces)
    per, channels, _ = pieces[0].shape
    n1 = groups * per
    runs = list(tiles) * groups
    tile = lambda n: pl.BlockSpec((n, block, LANES), lambda i, ids: (0, i, 0))
    mine = lambda shape: pl.BlockSpec((1,) + shape[1:], lambda i, ids: (ids[0], 0, 0))
    names = ("fore", "rear", "twist", "inner", "inner_back")
    return pl.pallas_call(
        functools.partial(conv_kernel, groups),
        out_shape=[jax.ShapeDtypeStruct((n, channels, LANES), BF16) for n in runs],
        grid_spec=pltpu.PrefetchScalarGridSpec(
            num_scalar_prefetch=1,
            grid=(channels // block,),
            in_specs=[tile(per)] * groups
            + [pl.BlockSpec((block, n1, 2 * LANES), lambda i, ids: (i + first // block, 0, 0))]
            + [mine(tables[name].shape) for name in names[:2]]
            + [whole(tables[name].shape) for name in names[2:]],
            out_specs=[tile(n) for n in runs],
            scratch_shapes=[pltpu.VMEM((n1 * block, LANES), F32)] * 2,
        ),
        compiler_params=grant(14),
        name="conv",
    )(ids, *pieces, spec, *[tables[name] for name in names])


def query_kernel(query_ref, aux_ref, out_ref):
    aux = aux_ref[...]
    query = short_conv(query_ref[...].astype(F32), aux[:, 9:11], aux[:, 0:3])
    for j in range(out_ref.shape[0]):
        out_ref[j] = query[:, j * LANES : (j + 1) * LANES]


def query_conv(query_proj, aux):
    channels, tokens = query_proj.shape
    block = min(channels, 128)
    count = tokens // LANES
    return pl.pallas_call(
        query_kernel,
        out_shape=jax.ShapeDtypeStruct((count, channels, LANES), F32),
        grid=(channels // block,),
        in_specs=[
            pl.BlockSpec((block, tokens), lambda i: (i, 0)),
            pl.BlockSpec((block, aux.shape[1]), lambda i: (i, 0)),
        ],
        out_specs=pl.BlockSpec((count, block, LANES), lambda i: (0, i, 0)),
        compiler_params=grant(4),
        name="query",
    )(query_proj, aux)


def gate_kernel(chunk, chunks, tiles, ids_ref, *refs):
    pieces, (query_ref, left_ref, right_ref) = refs[:-3], refs[-3:]
    groups = len(pieces)
    rows = pieces[0].shape[1]
    for side, out_ref in enumerate((left_ref, right_ref)):

        @pl.when(lax.rem(pl.program_id(0), tiles) // (tiles // 2) == side)
        def _():
            for s, piece_ref in enumerate(pieces):
                group = lax.rem(ids_ref[0] + groups - s, groups)
                at = pl.ds(pl.multiple_of((group * chunks + chunk) * rows, rows), rows)
                to = pl.ds(pl.multiple_of(group * rows, rows), rows)
                conv = piece_ref[0].astype(F32)
                out_ref[to, :] = (query_ref[0, at, :] * conv).astype(BF16)


def gate(ids, pieces, query, chunk, chunks, start, tiles):
    groups = len(pieces)
    per, rows, _ = pieces[0].shape
    channels = query.shape[1]
    half = tiles // 2
    shape = (groups * rows, per // 2 * LANES)
    block = (groups * rows, LANES)
    left = lambda j, ids: (0, j // tiles * half + jnp.minimum(lax.rem(j, tiles), half - 1))
    right = lambda j, ids: (0, j // tiles * half + jnp.maximum(lax.rem(j, tiles) - half, 0))
    return pl.pallas_call(
        functools.partial(gate_kernel, chunk, chunks, tiles),
        out_shape=[jax.ShapeDtypeStruct(shape, BF16)] * 2,
        grid_spec=pltpu.PrefetchScalarGridSpec(
            num_scalar_prefetch=1,
            grid=(per,),
            in_specs=[pl.BlockSpec((1, rows, LANES), lambda j, ids: (j, 0, 0))] * groups
            + [pl.BlockSpec((1, channels, LANES), lambda j, ids: (start + j, 0, 0))],
            out_specs=[pl.BlockSpec(block, left), pl.BlockSpec(block, right)],
        ),
        compiler_params=grant(5),
        name="gate",
    )(ids, *pieces, query)


def turn_kernel(groups, chunks, ids_ref, weight_ref, *out_refs):
    rows = weight_ref.shape[0] // groups // chunks
    for at, out_ref in enumerate(out_refs):

        @pl.when(pl.program_id(0) == at)
        def _():
            parts = [
                weight_ref[(g * chunks + c) * rows : (g * chunks + c + 1) * rows, :]
                for c in range(chunks)
                for g in range(groups)
            ]
            out_ref[...] = jnp.concatenate(parts, axis=0).T


def turned(ids, out_weight, width, shards_of, groups, chunks):
    channels = out_weight.shape[0]
    step = min(width, 256)
    inner = width // step
    count = len(shards_of)

    def from_at(k, h, ids):
        shard = shards_of[0](ids)
        for at in range(1, count):
            shard = jnp.where(k == at, shards_of[at](ids), shard)
        return (0, shard * inner + h)

    def out_at(mine):
        return lambda k, h, ids: (
            jnp.where(k == mine, h, jnp.where(k < mine, 0, inner - 1)),
            0,
        )

    return pl.pallas_call(
        functools.partial(turn_kernel, groups, chunks),
        out_shape=[jax.ShapeDtypeStruct((width, channels), BF16)] * count,
        grid_spec=pltpu.PrefetchScalarGridSpec(
            num_scalar_prefetch=1,
            grid=(count, inner),
            in_specs=[pl.BlockSpec((channels, step), from_at)],
            out_specs=[pl.BlockSpec((step, channels), out_at(at)) for at in range(count)],
        ),
        compiler_params=grant(7),
        name="turn",
    )(ids, out_weight)


def project_kernel(slot, chunks, ids_ref, *refs):
    sources, refs = refs[: 4 * chunks], refs[4 * chunks :]
    weights, sides, outs = refs[0:2], (refs[2:4], refs[4:6]), refs[6:8]
    for colour in range(2):
        for partner in range(2):

            @pl.when((pl.program_id(0) == colour) & (((ids_ref[0] & 1) ^ slot) == partner))
            def _():
                total = None
                for near, table in enumerate((weights[colour], sides[colour][partner])):
                    stack = [sources[(2 * c + near) * 2 + colour][...] for c in range(chunks)]
                    term = dot(table[...], jnp.concatenate(stack, axis=0))
                    total = term if total is None else total + term
                outs[colour][...] = total.astype(BF16)


def project(ids, sources, weights, sides, slot, h):
    width, channels = weights[0].shape
    flat = [array for own, near in sources for array in (*own, *near)]
    tokens = min(array.shape[1] for array in flat)
    step = min(width, 512)
    inner = width // step

    def source(array):
        at = h if array.shape[1] > tokens else 0
        return pl.BlockSpec((array.shape[0], tokens), lambda *_: (0, at))

    def when(active, mine, colour, h):
        return (jnp.where(active, h, jnp.where(colour > mine, inner - 1, 0)), 0)

    def side_at(mine, partner):
        def at(colour, h, ids):
            chosen = ((ids[0] & 1) ^ slot) == partner
            return when((colour == mine) & chosen, mine, jnp.where(chosen, colour, mine), h)

        return at

    def colour_at(mine):
        return lambda colour, h, ids: when(colour == mine, mine, colour, h)

    return pl.pallas_call(
        functools.partial(project_kernel, slot, len(sources)),
        out_shape=[jax.ShapeDtypeStruct((width, tokens), BF16)] * 2,
        grid_spec=pltpu.PrefetchScalarGridSpec(
            num_scalar_prefetch=1,
            grid=(2, inner),
            in_specs=[source(array) for array in flat]
            + [pl.BlockSpec((step, channels), colour_at(colour)) for colour in range(2)]
            + [
                pl.BlockSpec((step, channels), side_at(colour, partner))
                for colour in range(2)
                for partner in range(2)
            ],
            out_specs=[pl.BlockSpec((step, tokens), colour_at(colour)) for colour in range(2)],
        ),
        compiler_params=grant(18),
        name="project",
    )(ids, *flat, *weights, *sides[0], *sides[1])


def medium_spectrum(taps, fore_ref):
    width = taps.shape[0]
    over_taps = (((0,), (0,)), ((), ()))
    spec = lax.dot_general(taps, fore_ref[:width], over_taps, preferred_element_type=F32)
    return spec[:, :width], spec[:, width:]


def medium_blocks(wide, ker_re, ker_im, fore_ref, back_ref):
    width = ker_re.shape[1]
    out = []
    for b in range(wide.shape[1] // width - 1):
        window = wide[:, b * width : (b + 2) * width]
        sig = dot(window, fore_ref[...])
        sig_re, sig_im = sig[:, :width], sig[:, width:]
        product = jnp.concatenate(
            [
                (sig_re * ker_re - sig_im * ker_im).astype(BF16),
                (sig_re * ker_im + sig_im * ker_re).astype(BF16),
            ],
            axis=1,
        )
        out.append(dot(product, back_ref[...]).astype(BF16))
    return jnp.concatenate(out, axis=1)


def joined(parts, counts):
    refs, out = list(parts), []
    for count in counts:
        total = refs.pop(0)[...].astype(F32)
        for _ in range(count - 1):
            total = total + refs.pop(0)[...].astype(F32)
        out.append(total.astype(BF16))
    return jnp.concatenate(out, axis=1)


def late_kernel(counts, *refs):
    n = sum(counts)
    taps_ref, fore_ref, back_ref, oper_ref, edge_ref, out_ref = refs[n:]
    value = joined(refs[:n], counts)
    oper_ref[...] = value
    edge_ref[...] = value[:, -edge_ref.shape[1] :]
    ker_re, ker_im = medium_spectrum(taps_ref[...], fore_ref)
    out_ref[...] = medium_blocks(value, ker_re, ker_im, fore_ref, back_ref)


def early_kernel(counts, *refs):
    n = sum(counts)
    edge_ref, later_ref, tail_ref, taps_ref, fore_ref, back_ref, oper_ref, out_ref = refs[
        n:
    ]
    value = joined(refs[:n], counts)
    later = later_ref[...]
    half = value.shape[1]
    oper_ref[:, :half] = value
    oper_ref[:, half:] = later
    ker_re, ker_im = medium_spectrum(taps_ref[...], fore_ref)
    width = ker_re.shape[1]
    wide = jnp.concatenate([edge_ref[...], value, later[:, :width]], axis=1)
    out_ref[:, : half + width] = medium_blocks(wide, ker_re, ker_im, fore_ref, back_ref)
    out_ref[:, half + width :] = tail_ref[...]


def medium_call(kernel, parts, extra, taps, tables, widths):
    counts = tuple(len(p) for p in parts)
    arrays = [array for part in parts for array in part] + list(extra)
    channels = arrays[0].shape[0]
    width = taps.shape[0]
    block = min(channels, 256)
    row = lambda n: pl.BlockSpec((block, n), lambda i: (i, 0))
    return pl.pallas_call(
        functools.partial(kernel, counts),
        out_shape=[jax.ShapeDtypeStruct((channels, n), BF16) for n in widths],
        grid=(channels // block,),
        in_specs=[row(array.shape[1]) for array in arrays]
        + [pl.BlockSpec((width, block), lambda i: (0, i))]
        + [whole(t.shape) for t in tables],
        out_specs=[row(n) for n in widths],
        compiler_params=grant(10),
    )(*arrays, taps, *tables)


def ring(block, axis, distance):
    count = lax.axis_size(axis)
    if distance == 0:
        return block
    return lax.ppermute(block, axis, [(i, (i + distance) % count) for i in range(count)])


def forward(block, axis):
    count = lax.axis_size(axis)
    return lax.ppermute(block, axis, [(i, i + 1) for i in range(count - 1)])


def swapped(block, axis, bit):
    return lax.ppermute(block, axis, [(i, i ^ bit) for i in range(lax.axis_size(axis))])


def neighbour_weights(ids, out_weight, width, groups, chunks):
    slabs = turned(
        ids,
        out_weight,
        width,
        (lambda ids: ids[1] ^ 1 ^ ((ids[0] & 1) * 2), lambda ids: ids[1] ^ 2 ^ (ids[0] & 1)),
        groups,
        chunks,
    )
    return [swapped(slabs[0], "tp", 1), swapped(slabs[1], "tp", 2)]


def both_cores(sides, after):
    held = lax.optimization_barrier((*sides, after))
    out = []
    for straight in held[:2]:
        out.append((straight, swapped(straight, "ctx", 1)))
    return out, held[2]


def neighbours(gated):
    return [swapped(gated[0], "tp", 1), swapped(gated[1], "tp", 2)]


def shards(query_proj, key_proj, value_proj, short_taps, long_filter, out_weight, medium_taps):
    channels, tokens = query_proj.shape
    groups = lax.axis_size("ctx")
    length = long_filter.shape[1]
    tables = long_tables(length, groups)
    ids = jnp.stack([lax.axis_index("ctx"), lax.axis_index("tp")]).astype(jnp.int32)
    tails = [x[:, -2:] for x in (query_proj, key_proj, value_proj)]
    edges = forward(jnp.concatenate(tails, axis=1), "ctx").astype(F32)
    flat_taps = short_taps.reshape(9, channels).T
    aux = jnp.concatenate([flat_taps, edges, jnp.zeros((channels, 1), F32)], axis=1)
    owned = long_filter.shape[0]
    four = lax.axis_size("tp") == 4
    chunks = 2 if four and owned % 32 == 0 else 1
    rows = owned // chunks
    spec = spectra(long_filter, tables, min(owned, 16))
    sent = []
    for c in range(chunks):
        sent.append(list(mix(ids, key_proj, value_proj, aux, groups, c, chunks)))
    sides, weights = None, None
    if four:
        part = out_weight.shape[1] // 4
        held = lax.optimization_barrier((out_weight, sent[-1][0]))
        sent[-1][0] = held[1]
        sides = neighbour_weights(ids, held[0], part, groups, chunks)
        weights = turned(
            ids,
            held[0],
            part,
            (lambda ids: ids[1], lambda ids: ids[1] ^ 1, lambda ids: ids[1] ^ 2),
            groups,
            chunks,
        )
    query = query_conv(query_proj, aux)
    count = tokens // LANES
    half_tiles = count // 2
    own = {0: [], 1: []}
    near = {0: [], 1: []}
    for c in range(chunks):
        last = c == chunks - 1
        got = [ring(piece, "ctx", s) for s, piece in enumerate(sent[c])]
        runs = (half_tiles, half_tiles) if last else (count,)
        results = list(long_conv(ids, got, spec, tables, min(rows, 32), runs, c * rows))
        for h in (1, 0) if last else (None,):
            back = [
                ring(piece, "ctx", s)
                for s, piece in enumerate(results[h::2] if last else results)
            ]
            start = h * half_tiles if last else 0
            gated = list(gate(ids, back, query, c, chunks, start, half_tiles))
            if four and c == 0 and h != 0:
                sides, gated[0] = both_cores(sides, gated[0])
            beside = neighbours(gated) if four else None
            for at in (h,) if last else (0, 1):
                own[at].append(gated)
                near[at].append(beside)
    parts = {}
    for h in (1, 0):
        if not four:
            source = jnp.concatenate(own[h][0], axis=1)
            partial = lax.dot_general(
                out_weight, source, (((0,), (0,)), ((), ())), preferred_element_type=F32
            ).astype(BF16)
            parts[h] = [[lax.psum_scatter(partial, "tp", scatter_dimension=0, tiled=True)]]
            continue
        sources = list(zip(own[h], near[h]))
        send = project(ids, sources, (weights[2], weights[1]), sides, 1, h)
        got = [swapped(send[0], "tp", 2), swapped(send[1], "tp", 1)]
        keep = project(ids, sources, (weights[0], weights[0]), sides, 0, h)
        parts[h] = [[keep[0], got[0]], [keep[1], got[1]]]
    width = medium_taps.shape[0]
    half = tokens // 2
    tables = medium_tables(width)
    later, edge, tail = medium_call(
        late_kernel, parts[1], (), medium_taps, tables, (half, width, half - width)
    )
    edge = forward(edge, "ctx")
    return tuple(
        medium_call(
            early_kernel, parts[0], (edge, later, tail), medium_taps, tables, (tokens, tokens)
        )
    )


def solution(mesh):
    in_specs = (
        P("tp", "ctx"),
        P("tp", "ctx"),
        P("tp", "ctx"),
        P(None, None, "tp"),
        P(("tp", "ctx"), None),
        P("tp", None),
        P(None, "tp"),
    )
    out_specs = (P("tp", "ctx"), P("tp", "ctx"))
    return jax.shard_map(shards, mesh=mesh, in_specs=in_specs, out_specs=out_specs, check_vma=False)
```

```python
import functools
import math

import jax
import jax.numpy as jnp
import numpy as np
from jax import lax
from jax.experimental import pallas as pl
from jax.experimental.pallas import tpu as pltpu
from jax.sharding import PartitionSpec as P


LANES = 128
BF16 = jnp.bfloat16
F32 = jnp.float32


def split_table(table):
    high = np.asarray(table, np.float32).astype(BF16)
    low = (np.asarray(table, np.float64) - high.astype(np.float64)).astype(BF16)
    return high, low


def rotation(rows, cols, period):
    angles = 2.0 * math.pi * np.outer(rows, cols) / period
    return np.cos(angles), np.sin(angles)


@functools.lru_cache
def long_tables(length, groups):
    n1 = length // LANES
    first = np.arange(n1)
    lanes = np.arange(LANES)
    cos1, sin1 = rotation(first + 0.25, first, n1)
    outer = np.concatenate([cos1, -sin1], axis=0)
    back = np.concatenate([cos1.T, -sin1.T], axis=1) / n1
    twist_re, twist_im = rotation(first + 0.25, lanes, length)
    cos2, sin2 = rotation(lanes, lanes, LANES)
    inner = np.block([[cos2, -sin2], [sin2, cos2]])
    inner_back = np.block([[cos2, sin2], [-sin2, cos2]]) / LANES
    per = n1 // groups
    fore, rear = [], []
    for me in range(groups):
        ids, out = (me - np.arange(groups)) % groups, (me + np.arange(groups)) % groups
        ids = (ids[:, None] * per + np.arange(per)).reshape(-1)
        out = (out[:, None] * per + np.arange(per)).reshape(-1)
        high, low = split_table(outer[:, ids])
        fore.append(np.concatenate([high, low], axis=1))
        high, low = split_table(back[out])
        rear.append(np.concatenate([high, low], axis=1))
    high, low = split_table(outer)
    plain = np.concatenate([high, high, low], axis=1)
    twist = np.stack([twist_re, -twist_im]).astype(np.float32)
    inner_high = split_table(inner)[0]
    return dict(
        fore=np.stack(fore),
        rear=np.stack(rear),
        plain=plain,
        twist=twist,
        inner=inner_high,
        inner_back=split_table(inner_back)[0],
    )


@functools.lru_cache
def medium_tables(width):
    span = 2 * width
    cos, sin = rotation(np.arange(span), np.arange(width) + 0.5, span)
    fore = split_table(np.concatenate([cos, -sin], axis=1))[0]
    last = slice(width, span)
    back = np.concatenate([cos[last].T, -sin[last].T], axis=0) / width
    return fore, split_table(back)[0]


def grant(mib):
    return pltpu.CompilerParams(vmem_limit_bytes=mib * 1024 * 1024)


def dot(left, right):
    return jnp.dot(left, right, preferred_element_type=F32)


def short_conv(block, edge, taps):
    lane = lax.broadcasted_iota(jnp.int32, block.shape, 1)
    older, newer = edge[:, 0:1], edge[:, 1:2]
    back1 = jnp.where(lane == 0, newer, pltpu.roll(block, 1, 1))
    back2 = jnp.where(lane == 0, older, jnp.where(lane == 1, newer, pltpu.roll(block, 2, 1)))
    return taps[:, 0:1] * block + taps[:, 1:2] * back1 + taps[:, 2:3] * back2


def tail_kernel(*refs):
    *ins, out_ref = refs
    rows = [ref[...].astype(F32).T[-2:] for ref in ins]
    rows.append(jnp.zeros((out_ref.shape[0] - 2 * len(ins), out_ref.shape[1]), F32))
    out_ref[...] = jnp.concatenate(rows, axis=0).astype(BF16)


def tails(arrays):
    channels, tokens = arrays[0].shape
    last = pl.BlockSpec((channels, LANES), lambda i: (0, tokens // LANES - 1))
    return pl.pallas_call(
        tail_kernel,
        out_shape=jax.ShapeDtypeStruct((8, channels), BF16),
        grid=(1,),
        in_specs=[last] * len(arrays),
        out_specs=whole((8, channels)),
        name="tails",
    )(*arrays)


def mix_kernel(ids_ref, key_ref, value_ref, aux_ref, *out_refs):
    aux = aux_ref[...]
    keys = short_conv(key_ref[...].astype(F32), aux[:, 11:13], aux[:, 3:6])
    values = short_conv(value_ref[...].astype(F32), aux[:, 13:15], aux[:, 6:9])
    mixed = (keys * values).astype(BF16)

    for at, out_ref in enumerate(out_refs):

        @pl.when(pl.program_id(0) == at)
        def _():
            for j in range(out_ref.shape[0]):
                out_ref[j] = mixed[:, j * LANES : (j + 1) * LANES]


def mix(ids, key_proj, value_proj, aux, groups, chunk, chunks):
    channels, tokens = key_proj.shape
    rows = channels // groups // chunks
    count = tokens // LANES

    where = lambda g, ids: (lax.rem(ids[0] + g, groups) * chunks + chunk, 0)
    return pl.pallas_call(
        mix_kernel,
        out_shape=[jax.ShapeDtypeStruct((count, rows, LANES), BF16)] * groups,
        grid_spec=pltpu.PrefetchScalarGridSpec(
            num_scalar_prefetch=1,
            grid=(groups,),
            in_specs=[
                pl.BlockSpec((rows, tokens), where),
                pl.BlockSpec((rows, tokens), where),
                pl.BlockSpec((rows, aux.shape[1]), where),
            ],
            out_specs=[whole((count, rows, LANES))] * groups,
        ),
        compiler_params=grant(6),
        name="mix",
    )(ids, key_proj, value_proj, aux)


def twisted(wide, twist_re, twist_im, count):
    half = wide.shape[0] // 2
    out = []
    for c in range(count):
        re = wide[:half, c * LANES : (c + 1) * LANES]
        im = wide[half:, c * LANES : (c + 1) * LANES]
        out.append((re * twist_re - im * twist_im, re * twist_im + im * twist_re))
    return out


def filter_kernel(filter_ref, plain_ref, twist_ref, inner_ref, out_ref, rows_ref):
    block = filter_ref.shape[0]
    n1 = filter_ref.shape[1] // LANES
    for n in range(n1):
        rows_ref[n * block : (n + 1) * block, :] = filter_ref[:, n * LANES : (n + 1) * LANES]

    group = math.gcd(block, 8)

    def body(at, carry):
        base = at * group
        lines = []
        for pair in range(group // 2):
            loaded = [
                rows_ref[pl.ds(base + 2 * pair + c, n1, stride=block), :] for c in range(2)
            ]
            both = jnp.concatenate(loaded, axis=1)
            high = both.astype(BF16)
            low = (both - high.astype(F32)).astype(BF16)
            wide = dot(plain_ref[...], jnp.concatenate([high, low, high], axis=0))
            for re, im in twisted(wide, twist_ref[0], twist_ref[1], 2):
                lines.append(jnp.concatenate([re.astype(BF16), im.astype(BF16)], axis=1))
        spectrum = dot(jnp.concatenate(lines, axis=0), inner_ref[...])
        out_ref[pl.ds(base, group)] = spectrum.reshape(group, n1, 2 * LANES)
        return carry

    lax.fori_loop(0, block // group, body, 0, unroll=2)


def whole(shape):
    return pl.BlockSpec(shape, lambda *_: (0,) * len(shape))


def spectra(long_filter, tables, block):
    channels, length = long_filter.shape
    n1 = length // LANES
    names = ("plain", "twist", "inner")
    return pl.pallas_call(
        filter_kernel,
        out_shape=jax.ShapeDtypeStruct((channels, n1, 2 * LANES), F32),
        grid=(channels // block,),
        in_specs=[pl.BlockSpec((block, length), lambda i: (i, 0))]
        + [whole(tables[name].shape) for name in names],
        out_specs=pl.BlockSpec((block, n1, 2 * LANES), lambda i: (i, 0, 0)),
        scratch_shapes=[pltpu.VMEM((n1 * block, LANES), F32)],
        compiler_params=grant(9),
        name="spectra",
    )(long_filter, *[tables[name] for name in names])


def conv_kernel(count, ids_ref, *refs):
    pieces = refs[:count]
    spec_ref, fore_ref, rear_ref, twist_ref, inner_ref, back_ref = refs[count : count + 6]
    outs, (rows_ref, done_ref) = refs[count + 6 : -2], refs[-2:]
    per, block, _ = pieces[0].shape
    at = 0
    for piece_ref in pieces:
        size = per * block
        rows_ref[at : at + size, :] = piece_ref[...].astype(F32).reshape(size, LANES)
        at += size
    n1 = at // block
    group = math.gcd(block, 8)

    def body(at, carry):
        base = at * group
        lines = []
        for pair in range(group // 2):
            loaded = [
                rows_ref[pl.ds(base + 2 * pair + c, n1, stride=block), :].astype(BF16)
                for c in range(2)
            ]
            both = jnp.concatenate(loaded, axis=1)
            wide = dot(fore_ref[0], jnp.concatenate([both, both], axis=0))
            for re, im in twisted(wide, twist_ref[0], twist_ref[1], 2):
                lines.append(jnp.concatenate([re.astype(BF16), im.astype(BF16)], axis=1))
        spectrum = dot(jnp.concatenate(lines, axis=0), inner_ref[...])
        other = spec_ref[pl.ds(base, group)].reshape(group * n1, 2 * LANES)
        sig_re, sig_im = spectrum[:, :LANES], spectrum[:, LANES:]
        ker_re, ker_im = other[:, :LANES], other[:, LANES:]
        product = jnp.concatenate(
            [
                (sig_re * ker_re - sig_im * ker_im).astype(BF16),
                (sig_re * ker_im + sig_im * ker_re).astype(BF16),
            ],
            axis=1,
        )
        turned = dot(product, back_ref[...])
        for pair in range(group // 2):
            stacks = []
            for c in range(2):
                at_row = (2 * pair + c) * n1
                re = turned[at_row : at_row + n1, :LANES]
                im = turned[at_row : at_row + n1, LANES:]
                top = (re * twist_ref[0] + im * twist_ref[1]).astype(BF16)
                low = (im * twist_ref[0] - re * twist_ref[1]).astype(BF16)
                stacks.append(jnp.concatenate([top, low, top, low], axis=0))
            result = dot(rear_ref[0], jnp.concatenate(stacks, axis=1))
            for c in range(2):
                done_ref[pl.ds(base + 2 * pair + c, n1, stride=block), :] = result[
                    :, c * LANES : (c + 1) * LANES
                ]
        return carry

    lax.fori_loop(0, block // group, body, 0, unroll=2)
    at = 0
    for out_ref in outs:
        size = math.prod(out_ref.shape[:-1])
        out_ref[...] = done_ref[at : at + size, :].reshape(out_ref.shape).astype(BF16)
        at += size


def long_conv(ids, pieces, spec, tables, block, tiles, first):
    groups = len(pieces)
    per, channels, _ = pieces[0].shape
    n1 = groups * per
    runs = list(tiles) * groups
    tile = lambda n: pl.BlockSpec((n, block, LANES), lambda i, ids: (0, i, 0))
    mine = lambda shape: pl.BlockSpec((1,) + shape[1:], lambda i, ids: (ids[0], 0, 0))
    names = ("fore", "rear", "twist", "inner", "inner_back")
    return pl.pallas_call(
        functools.partial(conv_kernel, groups),
        out_shape=[jax.ShapeDtypeStruct((n, channels, LANES), BF16) for n in runs],
        grid_spec=pltpu.PrefetchScalarGridSpec(
            num_scalar_prefetch=1,
            grid=(channels // block,),
            in_specs=[tile(per)] * groups
            + [pl.BlockSpec((block, n1, 2 * LANES), lambda i, ids: (i + first // block, 0, 0))]
            + [mine(tables[name].shape) for name in names[:2]]
            + [whole(tables[name].shape) for name in names[2:]],
            out_specs=[tile(n) for n in runs],
            scratch_shapes=[pltpu.VMEM((n1 * block, LANES), F32)] * 2,
        ),
        compiler_params=grant(14),
        name="conv",
    )(ids, *pieces, spec, *[tables[name] for name in names])


def query_kernel(query_ref, aux_ref, out_ref):
    aux = aux_ref[...]
    query = short_conv(query_ref[...].astype(F32), aux[:, 9:11], aux[:, 0:3])
    for j in range(out_ref.shape[0]):
        out_ref[j] = query[:, j * LANES : (j + 1) * LANES]


def query_conv(query_proj, aux):
    channels, tokens = query_proj.shape
    block = min(channels, 128)
    count = tokens // LANES
    return pl.pallas_call(
        query_kernel,
        out_shape=jax.ShapeDtypeStruct((count, channels, LANES), F32),
        grid=(channels // block,),
        in_specs=[
            pl.BlockSpec((block, tokens), lambda i: (i, 0)),
            pl.BlockSpec((block, aux.shape[1]), lambda i: (i, 0)),
        ],
        out_specs=pl.BlockSpec((count, block, LANES), lambda i: (0, i, 0)),
        compiler_params=grant(4),
        name="query",
    )(query_proj, aux)


def gate_kernel(chunk, chunks, tiles, ids_ref, *refs):
    pieces, (query_ref, left_ref, right_ref) = refs[:-3], refs[-3:]
    groups = len(pieces)
    rows = pieces[0].shape[1]
    for side, out_ref in enumerate((left_ref, right_ref)):

        @pl.when(lax.rem(pl.program_id(0), tiles) // (tiles // 2) == side)
        def _():
            for s, piece_ref in enumerate(pieces):
                group = lax.rem(ids_ref[0] + groups - s, groups)
                at = pl.ds(pl.multiple_of((group * chunks + chunk) * rows, rows), rows)
                to = pl.ds(pl.multiple_of(group * rows, rows), rows)
                conv = piece_ref[0].astype(F32)
                out_ref[to, :] = (query_ref[0, at, :] * conv).astype(BF16)


def gate(ids, pieces, query, chunk, chunks, start, tiles):
    groups = len(pieces)
    per, rows, _ = pieces[0].shape
    channels = query.shape[1]
    half = tiles // 2
    shape = (groups * rows, per // 2 * LANES)
    block = (groups * rows, LANES)
    left = lambda j, ids: (0, j // tiles * half + jnp.minimum(lax.rem(j, tiles), half - 1))
    right = lambda j, ids: (0, j // tiles * half + jnp.maximum(lax.rem(j, tiles) - half, 0))
    return pl.pallas_call(
        functools.partial(gate_kernel, chunk, chunks, tiles),
        out_shape=[jax.ShapeDtypeStruct(shape, BF16)] * 2,
        grid_spec=pltpu.PrefetchScalarGridSpec(
            num_scalar_prefetch=1,
            grid=(per,),
            in_specs=[pl.BlockSpec((1, rows, LANES), lambda j, ids: (j, 0, 0))] * groups
            + [pl.BlockSpec((1, channels, LANES), lambda j, ids: (start + j, 0, 0))],
            out_specs=[pl.BlockSpec(block, left), pl.BlockSpec(block, right)],
        ),
        compiler_params=grant(5),
        name="gate",
    )(ids, *pieces, query)


def turn_kernel(groups, chunks, ids_ref, weight_ref, *out_refs):
    rows = weight_ref.shape[0] // groups // chunks
    for at, out_ref in enumerate(out_refs):

        @pl.when(pl.program_id(0) == at)
        def _():
            parts = [
                weight_ref[(g * chunks + c) * rows : (g * chunks + c + 1) * rows, :]
                for c in range(chunks)
                for g in range(groups)
            ]
            out_ref[...] = jnp.concatenate(parts, axis=0).T


def turned(ids, out_weight, width, shards_of, groups, chunks):
    channels = out_weight.shape[0]
    step = min(width, 256)
    inner = width // step
    count = len(shards_of)

    def from_at(k, h, ids):
        shard = shards_of[0](ids)
        for at in range(1, count):
            shard = jnp.where(k == at, shards_of[at](ids), shard)
        return (0, shard * inner + h)

    def out_at(mine):
        return lambda k, h, ids: (
            jnp.where(k == mine, h, jnp.where(k < mine, 0, inner - 1)),
            0,
        )

    return pl.pallas_call(
        functools.partial(turn_kernel, groups, chunks),
        out_shape=[jax.ShapeDtypeStruct((width, channels), BF16)] * count,
        grid_spec=pltpu.PrefetchScalarGridSpec(
            num_scalar_prefetch=1,
            grid=(count, inner),
            in_specs=[pl.BlockSpec((channels, step), from_at)],
            out_specs=[pl.BlockSpec((step, channels), out_at(at)) for at in range(count)],
        ),
        compiler_params=grant(7),
        name="turn",
    )(ids, out_weight)


def project_kernel(slot, chunks, ids_ref, *refs):
    sources, refs = refs[: 4 * chunks], refs[4 * chunks :]
    weights, sides, outs = refs[0:2], (refs[2:4], refs[4:6]), refs[6:8]
    for colour in range(2):
        for partner in range(2):

            @pl.when((pl.program_id(0) == colour) & (((ids_ref[0] & 1) ^ slot) == partner))
            def _():
                total = None
                for near, table in enumerate((weights[colour], sides[colour][partner])):
                    stack = [sources[(2 * c + near) * 2 + colour][...] for c in range(chunks)]
                    term = dot(table[...], jnp.concatenate(stack, axis=0))
                    total = term if total is None else total + term
                outs[colour][...] = total.astype(BF16)


def project(ids, sources, weights, sides, slot, h):
    width, channels = weights[0].shape
    flat = [array for own, near in sources for array in (*own, *near)]
    tokens = min(array.shape[1] for array in flat)
    step = min(width, 512)
    inner = width // step

    def source(array):
        at = h if array.shape[1] > tokens else 0
        return pl.BlockSpec((array.shape[0], tokens), lambda *_: (0, at))

    def when(active, mine, colour, h):
        return (jnp.where(active, h, jnp.where(colour > mine, inner - 1, 0)), 0)

    def side_at(mine, partner):
        def at(colour, h, ids):
            chosen = ((ids[0] & 1) ^ slot) == partner
            return when((colour == mine) & chosen, mine, jnp.where(chosen, colour, mine), h)

        return at

    def colour_at(mine):
        return lambda colour, h, ids: when(colour == mine, mine, colour, h)

    return pl.pallas_call(
        functools.partial(project_kernel, slot, len(sources)),
        out_shape=[jax.ShapeDtypeStruct((width, tokens), BF16)] * 2,
        grid_spec=pltpu.PrefetchScalarGridSpec(
            num_scalar_prefetch=1,
            grid=(2, inner),
            in_specs=[source(array) for array in flat]
            + [pl.BlockSpec((step, channels), colour_at(colour)) for colour in range(2)]
            + [
                pl.BlockSpec((step, channels), side_at(colour, partner))
                for colour in range(2)
                for partner in range(2)
            ],
            out_specs=[pl.BlockSpec((step, tokens), colour_at(colour)) for colour in range(2)],
        ),
        compiler_params=grant(18),
        name="project",
    )(ids, *flat, *weights, *sides[0], *sides[1])


def medium_spectrum(taps, fore_ref):
    width = taps.shape[0]
    over_taps = (((0,), (0,)), ((), ()))
    spec = lax.dot_general(taps, fore_ref[:width], over_taps, preferred_element_type=F32)
    return spec[:, :width], spec[:, width:]


def medium_blocks(wide, ker_re, ker_im, fore_ref, back_ref):
    width = ker_re.shape[1]
    out = []
    for b in range(wide.shape[1] // width - 1):
        window = wide[:, b * width : (b + 2) * width]
        sig = dot(window, fore_ref[...])
        sig_re, sig_im = sig[:, :width], sig[:, width:]
        product = jnp.concatenate(
            [
                (sig_re * ker_re - sig_im * ker_im).astype(BF16),
                (sig_re * ker_im + sig_im * ker_re).astype(BF16),
            ],
            axis=1,
        )
        out.append(dot(product, back_ref[...]).astype(BF16))
    return jnp.concatenate(out, axis=1)


def joined(parts, counts):
    refs, out = list(parts), []
    for count in counts:
        total = refs.pop(0)[...].astype(F32)
        for _ in range(count - 1):
            total = total + refs.pop(0)[...].astype(F32)
        out.append(total.astype(BF16))
    return jnp.concatenate(out, axis=1)


def late_kernel(counts, *refs):
    n = sum(counts)
    taps_ref, fore_ref, back_ref, oper_ref, edge_ref, out_ref = refs[n:]
    value = joined(refs[:n], counts)
    oper_ref[...] = value
    edge_ref[...] = value[:, -edge_ref.shape[1] :]
    ker_re, ker_im = medium_spectrum(taps_ref[...], fore_ref)
    out_ref[...] = medium_blocks(value, ker_re, ker_im, fore_ref, back_ref)


def early_kernel(counts, *refs):
    n = sum(counts)
    edge_ref, later_ref, tail_ref, taps_ref, fore_ref, back_ref, oper_ref, out_ref = refs[
        n:
    ]
    value = joined(refs[:n], counts)
    later = later_ref[...]
    half = value.shape[1]
    oper_ref[:, :half] = value
    oper_ref[:, half:] = later
    ker_re, ker_im = medium_spectrum(taps_ref[...], fore_ref)
    width = ker_re.shape[1]
    wide = jnp.concatenate([edge_ref[...], value, later[:, :width]], axis=1)
    out_ref[:, : half + width] = medium_blocks(wide, ker_re, ker_im, fore_ref, back_ref)
    out_ref[:, half + width :] = tail_ref[...]


def medium_call(kernel, parts, extra, taps, tables, widths):
    counts = tuple(len(p) for p in parts)
    arrays = [array for part in parts for array in part] + list(extra)
    channels = arrays[0].shape[0]
    width = taps.shape[0]
    block = min(channels, 256)
    row = lambda n: pl.BlockSpec((block, n), lambda i: (i, 0))
    return pl.pallas_call(
        functools.partial(kernel, counts),
        out_shape=[jax.ShapeDtypeStruct((channels, n), BF16) for n in widths],
        grid=(channels // block,),
        in_specs=[row(array.shape[1]) for array in arrays]
        + [pl.BlockSpec((width, block), lambda i: (0, i))]
        + [whole(t.shape) for t in tables],
        out_specs=[row(n) for n in widths],
        compiler_params=grant(10),
    )(*arrays, taps, *tables)


def ring(block, axis, distance):
    count = lax.axis_size(axis)
    if distance == 0:
        return block
    return lax.ppermute(block, axis, [(i, (i + distance) % count) for i in range(count)])


def forward(block, axis):
    count = lax.axis_size(axis)
    return lax.ppermute(block, axis, [(i, i + 1) for i in range(count - 1)])


def swapped(block, axis, bit):
    return lax.ppermute(block, axis, [(i, i ^ bit) for i in range(lax.axis_size(axis))])


def neighbour_weights(ids, out_weight, width, groups, chunks):
    slabs = turned(
        ids,
        out_weight,
        width,
        (lambda ids: ids[1] ^ 1 ^ ((ids[0] & 1) * 2), lambda ids: ids[1] ^ 2 ^ (ids[0] & 1)),
        groups,
        chunks,
    )
    return [swapped(slabs[0], "tp", 1), swapped(slabs[1], "tp", 2)]


def both_cores(sides, after):
    held = lax.optimization_barrier((*sides, after))
    out = []
    for straight in held[:2]:
        out.append((straight, swapped(straight, "ctx", 1)))
    return out, held[2]


def neighbours(gated):
    return [swapped(gated[0], "tp", 1), swapped(gated[1], "tp", 2)]


def shards(query_proj, key_proj, value_proj, short_taps, long_filter, out_weight, medium_taps):
    channels, tokens = query_proj.shape
    groups = lax.axis_size("ctx")
    length = long_filter.shape[1]
    tables = long_tables(length, groups)
    ids = jnp.stack([lax.axis_index("ctx"), lax.axis_index("tp")]).astype(jnp.int32)
    edges = forward(tails((query_proj, key_proj, value_proj)), "ctx").astype(F32)
    aux = jnp.concatenate([short_taps.reshape(9, channels), edges[:7]], axis=0).T
    owned = long_filter.shape[0]
    four = lax.axis_size("tp") == 4
    chunks = 2 if four and owned % 32 == 0 else 1
    rows = owned // chunks
    spec = spectra(long_filter, tables, min(owned, 16))
    sent = []
    for c in range(chunks):
        sent.append(list(mix(ids, key_proj, value_proj, aux, groups, c, chunks)))
    sides, weights = None, None
    if four:
        part = out_weight.shape[1] // 4
        held = lax.optimization_barrier((out_weight, sent[-1][0]))
        sent[-1][0] = held[1]
        sides = neighbour_weights(ids, held[0], part, groups, chunks)
        weights = turned(
            ids,
            held[0],
            part,
            (lambda ids: ids[1], lambda ids: ids[1] ^ 1, lambda ids: ids[1] ^ 2),
            groups,
            chunks,
        )
    query = query_conv(query_proj, aux)
    count = tokens // LANES
    half_tiles = count // 2
    own = {0: [], 1: []}
    near = {0: [], 1: []}
    for c in range(chunks):
        last = c == chunks - 1
        got = [ring(piece, "ctx", s) for s, piece in enumerate(sent[c])]
        runs = (half_tiles, half_tiles) if last else (count,)
        results = list(long_conv(ids, got, spec, tables, min(rows, 32), runs, c * rows))
        for h in (1, 0) if last else (None,):
            back = [
                ring(piece, "ctx", s)
                for s, piece in enumerate(results[h::2] if last else results)
            ]
            start = h * half_tiles if last else 0
            gated = list(gate(ids, back, query, c, chunks, start, half_tiles))
            if four and c == 0 and h != 0:
                sides, gated[0] = both_cores(sides, gated[0])
            beside = neighbours(gated) if four else None
            for at in (h,) if last else (0, 1):
                own[at].append(gated)
                near[at].append(beside)
    parts = {}
    for h in (1, 0):
        if not four:
            source = jnp.concatenate(own[h][0], axis=1)
            partial = lax.dot_general(
                out_weight, source, (((0,), (0,)), ((), ())), preferred_element_type=F32
            ).astype(BF16)
            parts[h] = [[lax.psum_scatter(partial, "tp", scatter_dimension=0, tiled=True)]]
            continue
        sources = list(zip(own[h], near[h]))
        send = project(ids, sources, (weights[2], weights[1]), sides, 1, h)
        got = [swapped(send[0], "tp", 2), swapped(send[1], "tp", 1)]
        keep = project(ids, sources, (weights[0], weights[0]), sides, 0, h)
        parts[h] = [[keep[0], got[0]], [keep[1], got[1]]]
    width = medium_taps.shape[0]
    half = tokens // 2
    tables = medium_tables(width)
    later, edge, tail = medium_call(
        late_kernel, parts[1], (), medium_taps, tables, (half, width, half - width)
    )
    edge = forward(edge, "ctx")
    return tuple(
        medium_call(
            early_kernel, parts[0], (edge, later, tail), medium_taps, tables, (tokens, tokens)
        )
    )


def solution(mesh):
    in_specs = (
        P("tp", "ctx"),
        P("tp", "ctx"),
        P("tp", "ctx"),
        P(None, None, "tp"),
        P(("tp", "ctx"), None),
        P("tp", None),
        P(None, "tp"),
    )
    out_specs = (P("tp", "ctx"), P("tp", "ctx"))
    return jax.shard_map(shards, mesh=mesh, in_specs=in_specs, out_specs=out_specs, check_vma=False)
```

```python
import functools
import math

import jax
import jax.numpy as jnp
import numpy as np
from jax import lax
from jax.experimental import pallas as pl
from jax.experimental.pallas import tpu as pltpu
from jax.sharding import PartitionSpec as P


LANES = 128
BF16 = jnp.bfloat16
F32 = jnp.float32


def split_table(table):
    high = np.asarray(table, np.float32).astype(BF16)
    low = (np.asarray(table, np.float64) - high.astype(np.float64)).astype(BF16)
    return high, low


def rotation(rows, cols, period):
    angles = 2.0 * math.pi * np.outer(rows, cols) / period
    return np.cos(angles), np.sin(angles)


@functools.lru_cache
def long_tables(length, groups):
    n1 = length // LANES
    first = np.arange(n1)
    lanes = np.arange(LANES)
    cos1, sin1 = rotation(first + 0.25, first, n1)
    outer = np.concatenate([cos1, -sin1], axis=0)
    back = np.concatenate([cos1.T, -sin1.T], axis=1) / n1
    twist_re, twist_im = rotation(first + 0.25, lanes, length)
    cos2, sin2 = rotation(lanes, lanes, LANES)
    inner = np.block([[cos2, -sin2], [sin2, cos2]])
    inner_back = np.block([[cos2, sin2], [-sin2, cos2]]) / LANES
    per = n1 // groups
    fore, rear = [], []
    for me in range(groups):
        ids, out = (me - np.arange(groups)) % groups, (me + np.arange(groups)) % groups
        ids = (ids[:, None] * per + np.arange(per)).reshape(-1)
        out = (out[:, None] * per + np.arange(per)).reshape(-1)
        high, low = split_table(outer[:, ids])
        fore.append(np.concatenate([high, low], axis=1))
        high, low = split_table(back[out])
        rear.append(np.concatenate([high, low], axis=1))
    high, low = split_table(outer)
    plain = np.concatenate([high, high, low], axis=1)
    twist = np.stack([twist_re, -twist_im]).astype(np.float32)
    inner_high = split_table(inner)[0]
    return dict(
        fore=np.stack(fore),
        rear=np.stack(rear),
        plain=plain,
        twist=twist,
        inner=inner_high,
        inner_back=split_table(inner_back)[0],
    )


@functools.lru_cache
def medium_tables(width):
    span = 2 * width
    cos, sin = rotation(np.arange(span), np.arange(width) + 0.5, span)
    fore = split_table(np.concatenate([cos, -sin], axis=1))[0]
    last = slice(width, span)
    back = np.concatenate([cos[last].T, -sin[last].T], axis=0) / width
    return fore, split_table(back)[0]


def grant(mib):
    return pltpu.CompilerParams(vmem_limit_bytes=mib * 1024 * 1024)


def dot(left, right):
    return jnp.dot(left, right, preferred_element_type=F32)


def short_conv(block, edge, taps):
    lane = lax.broadcasted_iota(jnp.int32, block.shape, 1)
    older, newer = edge[:, 0:1], edge[:, 1:2]
    back1 = jnp.where(lane == 0, newer, pltpu.roll(block, 1, 1))
    back2 = jnp.where(lane == 0, older, jnp.where(lane == 1, newer, pltpu.roll(block, 2, 1)))
    return taps[:, 0:1] * block + taps[:, 1:2] * back1 + taps[:, 2:3] * back2


def tail_kernel(*refs):
    *ins, out_ref = refs
    rows = [ref[...].astype(F32).T[-2:] for ref in ins]
    rows.append(jnp.zeros((out_ref.shape[0] - 2 * len(ins), out_ref.shape[1]), F32))
    out_ref[...] = jnp.concatenate(rows, axis=0).astype(BF16)


def tails(arrays):
    channels, tokens = arrays[0].shape
    last = pl.BlockSpec((channels, LANES), lambda i: (0, tokens // LANES - 1))
    return pl.pallas_call(
        tail_kernel,
        out_shape=jax.ShapeDtypeStruct((8, channels), BF16),
        grid=(1,),
        in_specs=[last] * len(arrays),
        out_specs=whole((8, channels)),
        name="tails",
    )(*arrays)


def mix_kernel(ids_ref, key_ref, value_ref, aux_ref, *out_refs):
    aux = aux_ref[...]
    keys = short_conv(key_ref[...].astype(F32), aux[:, 11:13], aux[:, 3:6])
    values = short_conv(value_ref[...].astype(F32), aux[:, 13:15], aux[:, 6:9])
    mixed = (keys * values).astype(BF16)

    for at, out_ref in enumerate(out_refs):

        @pl.when(pl.program_id(0) == at)
        def _():
            for j in range(out_ref.shape[0]):
                out_ref[j] = mixed[:, j * LANES : (j + 1) * LANES]


def mix(ids, key_proj, value_proj, aux, groups, chunk, chunks, first, number):
    channels, tokens = key_proj.shape
    rows = channels // groups // chunks
    count = tokens // LANES

    where = lambda g, ids: (lax.rem(ids[0] + first + g, groups) * chunks + chunk, 0)
    return pl.pallas_call(
        mix_kernel,
        out_shape=[jax.ShapeDtypeStruct((count, rows, LANES), BF16)] * number,
        grid_spec=pltpu.PrefetchScalarGridSpec(
            num_scalar_prefetch=1,
            grid=(number,),
            in_specs=[
                pl.BlockSpec((rows, tokens), where),
                pl.BlockSpec((rows, tokens), where),
                pl.BlockSpec((rows, aux.shape[1]), where),
            ],
            out_specs=[whole((count, rows, LANES))] * number,
        ),
        compiler_params=grant(6),
        name="mix",
    )(ids, key_proj, value_proj, aux)


def twisted(wide, twist_re, twist_im, count):
    half = wide.shape[0] // 2
    out = []
    for c in range(count):
        re = wide[:half, c * LANES : (c + 1) * LANES]
        im = wide[half:, c * LANES : (c + 1) * LANES]
        out.append((re * twist_re - im * twist_im, re * twist_im + im * twist_re))
    return out


def filter_kernel(filter_ref, plain_ref, twist_ref, inner_ref, out_ref, rows_ref):
    block = filter_ref.shape[0]
    n1 = filter_ref.shape[1] // LANES
    for n in range(n1):
        rows_ref[n * block : (n + 1) * block, :] = filter_ref[:, n * LANES : (n + 1) * LANES]

    group = math.gcd(block, 8)

    def body(at, carry):
        base = at * group
        lines = []
        for pair in range(group // 2):
            loaded = [
                rows_ref[pl.ds(base + 2 * pair + c, n1, stride=block), :] for c in range(2)
            ]
            both = jnp.concatenate(loaded, axis=1)
            high = both.astype(BF16)
            low = (both - high.astype(F32)).astype(BF16)
            wide = dot(plain_ref[...], jnp.concatenate([high, low, high], axis=0))
            for re, im in twisted(wide, twist_ref[0], twist_ref[1], 2):
                lines.append(jnp.concatenate([re.astype(BF16), im.astype(BF16)], axis=1))
        spectrum = dot(jnp.concatenate(lines, axis=0), inner_ref[...])
        out_ref[pl.ds(base, group)] = spectrum.reshape(group, n1, 2 * LANES)
        return carry

    lax.fori_loop(0, block // group, body, 0, unroll=2)


def whole(shape):
    return pl.BlockSpec(shape, lambda *_: (0,) * len(shape))


def spectra(long_filter, tables, block):
    channels, length = long_filter.shape
    n1 = length // LANES
    names = ("plain", "twist", "inner")
    return pl.pallas_call(
        filter_kernel,
        out_shape=jax.ShapeDtypeStruct((channels, n1, 2 * LANES), F32),
        grid=(channels // block,),
        in_specs=[pl.BlockSpec((block, length), lambda i: (i, 0))]
        + [whole(tables[name].shape) for name in names],
        out_specs=pl.BlockSpec((block, n1, 2 * LANES), lambda i: (i, 0, 0)),
        scratch_shapes=[pltpu.VMEM((n1 * block, LANES), F32)],
        compiler_params=grant(9),
        name="spectra",
    )(long_filter, *[tables[name] for name in names])


def conv_kernel(count, ids_ref, *refs):
    pieces = refs[:count]
    spec_ref, fore_ref, rear_ref, twist_ref, inner_ref, back_ref = refs[count : count + 6]
    outs, (rows_ref, done_ref) = refs[count + 6 : -2], refs[-2:]
    per, block, _ = pieces[0].shape
    at = 0
    for piece_ref in pieces:
        size = per * block
        rows_ref[at : at + size, :] = piece_ref[...].astype(F32).reshape(size, LANES)
        at += size
    n1 = at // block
    group = math.gcd(block, 8)

    def body(at, carry):
        base = at * group
        lines = []
        for pair in range(group // 2):
            loaded = [
                rows_ref[pl.ds(base + 2 * pair + c, n1, stride=block), :].astype(BF16)
                for c in range(2)
            ]
            both = jnp.concatenate(loaded, axis=1)
            wide = dot(fore_ref[0], jnp.concatenate([both, both], axis=0))
            for re, im in twisted(wide, twist_ref[0], twist_ref[1], 2):
                lines.append(jnp.concatenate([re.astype(BF16), im.astype(BF16)], axis=1))
        spectrum = dot(jnp.concatenate(lines, axis=0), inner_ref[...])
        other = spec_ref[pl.ds(base, group)].reshape(group * n1, 2 * LANES)
        sig_re, sig_im = spectrum[:, :LANES], spectrum[:, LANES:]
        ker_re, ker_im = other[:, :LANES], other[:, LANES:]
        product = jnp.concatenate(
            [
                (sig_re * ker_re - sig_im * ker_im).astype(BF16),
                (sig_re * ker_im + sig_im * ker_re).astype(BF16),
            ],
            axis=1,
        )
        turned = dot(product, back_ref[...])
        for pair in range(group // 2):
            stacks = []
            for c in range(2):
                at_row = (2 * pair + c) * n1
                re = turned[at_row : at_row + n1, :LANES]
                im = turned[at_row : at_row + n1, LANES:]
                top = (re * twist_ref[0] + im * twist_ref[1]).astype(BF16)
                low = (im * twist_ref[0] - re * twist_ref[1]).astype(BF16)
                stacks.append(jnp.concatenate([top, low, top, low], axis=0))
            result = dot(rear_ref[0], jnp.concatenate(stacks, axis=1))
            for c in range(2):
                done_ref[pl.ds(base + 2 * pair + c, n1, stride=block), :] = result[
                    :, c * LANES : (c + 1) * LANES
                ]
        return carry

    lax.fori_loop(0, block // group, body, 0, unroll=2)
    at = 0
    for out_ref in outs:
        size = math.prod(out_ref.shape[:-1])
        out_ref[...] = done_ref[at : at + size, :].reshape(out_ref.shape).astype(BF16)
        at += size


def long_conv(ids, pieces, spec, tables, block, tiles, first):
    groups = len(pieces)
    per, channels, _ = pieces[0].shape
    n1 = groups * per
    runs = list(tiles) * groups
    tile = lambda n: pl.BlockSpec((n, block, LANES), lambda i, ids: (0, i, 0))
    mine = lambda shape: pl.BlockSpec((1,) + shape[1:], lambda i, ids: (ids[0], 0, 0))
    names = ("fore", "rear", "twist", "inner", "inner_back")
    return pl.pallas_call(
        functools.partial(conv_kernel, groups),
        out_shape=[jax.ShapeDtypeStruct((n, channels, LANES), BF16) for n in runs],
        grid_spec=pltpu.PrefetchScalarGridSpec(
            num_scalar_prefetch=1,
            grid=(channels // block,),
            in_specs=[tile(per)] * groups
            + [pl.BlockSpec((block, n1, 2 * LANES), lambda i, ids: (i + first // block, 0, 0))]
            + [mine(tables[name].shape) for name in names[:2]]
            + [whole(tables[name].shape) for name in names[2:]],
            out_specs=[tile(n) for n in runs],
            scratch_shapes=[pltpu.VMEM((n1 * block, LANES), F32)] * 2,
        ),
        compiler_params=grant(14),
        name="conv",
    )(ids, *pieces, spec, *[tables[name] for name in names])


def query_kernel(query_ref, aux_ref, out_ref):
    aux = aux_ref[...]
    query = short_conv(query_ref[...].astype(F32), aux[:, 9:11], aux[:, 0:3])
    for j in range(out_ref.shape[0]):
        out_ref[j] = query[:, j * LANES : (j + 1) * LANES]


def query_conv(query_proj, aux):
    channels, tokens = query_proj.shape
    block = min(channels, 128)
    count = tokens // LANES
    return pl.pallas_call(
        query_kernel,
        out_shape=jax.ShapeDtypeStruct((count, channels, LANES), F32),
        grid=(channels // block,),
        in_specs=[
            pl.BlockSpec((block, tokens), lambda i: (i, 0)),
            pl.BlockSpec((block, aux.shape[1]), lambda i: (i, 0)),
        ],
        out_specs=pl.BlockSpec((count, block, LANES), lambda i: (0, i, 0)),
        compiler_params=grant(4),
        name="query",
    )(query_proj, aux)


def gate_kernel(chunk, chunks, tiles, ids_ref, *refs):
    pieces, (query_ref, left_ref, right_ref) = refs[:-3], refs[-3:]
    groups = len(pieces)
    rows = pieces[0].shape[1]
    for side, out_ref in enumerate((left_ref, right_ref)):

        @pl.when(lax.rem(pl.program_id(0), tiles) // (tiles // 2) == side)
        def _():
            for s, piece_ref in enumerate(pieces):
                group = lax.rem(ids_ref[0] + groups - s, groups)
                at = pl.ds(pl.multiple_of((group * chunks + chunk) * rows, rows), rows)
                to = pl.ds(pl.multiple_of(group * rows, rows), rows)
                conv = piece_ref[0].astype(F32)
                out_ref[to, :] = (query_ref[0, at, :] * conv).astype(BF16)


def gate(ids, pieces, query, chunk, chunks, start, tiles):
    groups = len(pieces)
    per, rows, _ = pieces[0].shape
    channels = query.shape[1]
    half = tiles // 2
    shape = (groups * rows, per // 2 * LANES)
    block = (groups * rows, LANES)
    left = lambda j, ids: (0, j // tiles * half + jnp.minimum(lax.rem(j, tiles), half - 1))
    right = lambda j, ids: (0, j // tiles * half + jnp.maximum(lax.rem(j, tiles) - half, 0))
    return pl.pallas_call(
        functools.partial(gate_kernel, chunk, chunks, tiles),
        out_shape=[jax.ShapeDtypeStruct(shape, BF16)] * 2,
        grid_spec=pltpu.PrefetchScalarGridSpec(
            num_scalar_prefetch=1,
            grid=(per,),
            in_specs=[pl.BlockSpec((1, rows, LANES), lambda j, ids: (j, 0, 0))] * groups
            + [pl.BlockSpec((1, channels, LANES), lambda j, ids: (start + j, 0, 0))],
            out_specs=[pl.BlockSpec(block, left), pl.BlockSpec(block, right)],
        ),
        compiler_params=grant(5),
        name="gate",
    )(ids, *pieces, query)


def turn_kernel(groups, chunks, ids_ref, weight_ref, *out_refs):
    rows = weight_ref.shape[0] // groups // chunks
    for at, out_ref in enumerate(out_refs):

        @pl.when(pl.program_id(0) == at)
        def _():
            parts = [
                weight_ref[(g * chunks + c) * rows : (g * chunks + c + 1) * rows, :]
                for c in range(chunks)
                for g in range(groups)
            ]
            out_ref[...] = jnp.concatenate(parts, axis=0).T


def turned(ids, out_weight, width, shards_of, groups, chunks):
    channels = out_weight.shape[0]
    step = min(width, 256)
    inner = width // step
    count = len(shards_of)

    def from_at(k, h, ids):
        shard = shards_of[0](ids)
        for at in range(1, count):
            shard = jnp.where(k == at, shards_of[at](ids), shard)
        return (0, shard * inner + h)

    def out_at(mine):
        return lambda k, h, ids: (
            jnp.where(k == mine, h, jnp.where(k < mine, 0, inner - 1)),
            0,
        )

    return pl.pallas_call(
        functools.partial(turn_kernel, groups, chunks),
        out_shape=[jax.ShapeDtypeStruct((width, channels), BF16)] * count,
        grid_spec=pltpu.PrefetchScalarGridSpec(
            num_scalar_prefetch=1,
            grid=(count, inner),
            in_specs=[pl.BlockSpec((channels, step), from_at)],
            out_specs=[pl.BlockSpec((step, channels), out_at(at)) for at in range(count)],
        ),
        compiler_params=grant(7),
        name="turn",
    )(ids, out_weight)


def project_kernel(slot, chunks, ids_ref, *refs):
    sources, refs = refs[: 4 * chunks], refs[4 * chunks :]
    weights, sides, outs = refs[0:2], (refs[2:4], refs[4:6]), refs[6:8]
    for colour in range(2):
        for partner in range(2):

            @pl.when((pl.program_id(0) == colour) & (((ids_ref[0] & 1) ^ slot) == partner))
            def _():
                total = None
                for near, table in enumerate((weights[colour], sides[colour][partner])):
                    stack = [sources[(2 * c + near) * 2 + colour][...] for c in range(chunks)]
                    term = dot(table[...], jnp.concatenate(stack, axis=0))
                    total = term if total is None else total + term
                outs[colour][...] = total.astype(BF16)


def project(ids, sources, weights, sides, slot, h):
    width, channels = weights[0].shape
    flat = [array for own, near in sources for array in (*own, *near)]
    tokens = min(array.shape[1] for array in flat)
    step = min(width, 512)
    inner = width // step

    def source(array):
        at = h if array.shape[1] > tokens else 0
        return pl.BlockSpec((array.shape[0], tokens), lambda *_: (0, at))

    def when(active, mine, colour, h):
        return (jnp.where(active, h, jnp.where(colour > mine, inner - 1, 0)), 0)

    def side_at(mine, partner):
        def at(colour, h, ids):
            chosen = ((ids[0] & 1) ^ slot) == partner
            return when((colour == mine) & chosen, mine, jnp.where(chosen, colour, mine), h)

        return at

    def colour_at(mine):
        return lambda colour, h, ids: when(colour == mine, mine, colour, h)

    return pl.pallas_call(
        functools.partial(project_kernel, slot, len(sources)),
        out_shape=[jax.ShapeDtypeStruct((width, tokens), BF16)] * 2,
        grid_spec=pltpu.PrefetchScalarGridSpec(
            num_scalar_prefetch=1,
            grid=(2, inner),
            in_specs=[source(array) for array in flat]
            + [pl.BlockSpec((step, channels), colour_at(colour)) for colour in range(2)]
            + [
                pl.BlockSpec((step, channels), side_at(colour, partner))
                for colour in range(2)
                for partner in range(2)
            ],
            out_specs=[pl.BlockSpec((step, tokens), colour_at(colour)) for colour in range(2)],
        ),
        compiler_params=grant(18),
        name="project",
    )(ids, *flat, *weights, *sides[0], *sides[1])


def medium_spectrum(taps, fore_ref):
    width = taps.shape[0]
    over_taps = (((0,), (0,)), ((), ()))
    spec = lax.dot_general(taps, fore_ref[:width], over_taps, preferred_element_type=F32)
    return spec[:, :width], spec[:, width:]


def medium_blocks(wide, ker_re, ker_im, fore_ref, back_ref):
    width = ker_re.shape[1]
    out = []
    for b in range(wide.shape[1] // width - 1):
        window = wide[:, b * width : (b + 2) * width]
        sig = dot(window, fore_ref[...])
        sig_re, sig_im = sig[:, :width], sig[:, width:]
        product = jnp.concatenate(
            [
                (sig_re * ker_re - sig_im * ker_im).astype(BF16),
                (sig_re * ker_im + sig_im * ker_re).astype(BF16),
            ],
            axis=1,
        )
        out.append(dot(product, back_ref[...]).astype(BF16))
    return jnp.concatenate(out, axis=1)


def joined(parts, counts):
    refs, out = list(parts), []
    for count in counts:
        total = refs.pop(0)[...].astype(F32)
        for _ in range(count - 1):
            total = total + refs.pop(0)[...].astype(F32)
        out.append(total.astype(BF16))
    return jnp.concatenate(out, axis=1)


def late_kernel(counts, *refs):
    n = sum(counts)
    taps_ref, fore_ref, back_ref, oper_ref, edge_ref, out_ref = refs[n:]
    value = joined(refs[:n], counts)
    oper_ref[...] = value
    edge_ref[...] = value[:, -edge_ref.shape[1] :]
    ker_re, ker_im = medium_spectrum(taps_ref[...], fore_ref)
    out_ref[...] = medium_blocks(value, ker_re, ker_im, fore_ref, back_ref)


def early_kernel(counts, *refs):
    n = sum(counts)
    edge_ref, later_ref, tail_ref, taps_ref, fore_ref, back_ref, oper_ref, out_ref = refs[
        n:
    ]
    value = joined(refs[:n], counts)
    later = later_ref[...]
    half = value.shape[1]
    oper_ref[:, :half] = value
    oper_ref[:, half:] = later
    ker_re, ker_im = medium_spectrum(taps_ref[...], fore_ref)
    width = ker_re.shape[1]
    wide = jnp.concatenate([edge_ref[...], value, later[:, :width]], axis=1)
    out_ref[:, : half + width] = medium_blocks(wide, ker_re, ker_im, fore_ref, back_ref)
    out_ref[:, half + width :] = tail_ref[...]


def medium_call(kernel, parts, extra, taps, tables, widths):
    counts = tuple(len(p) for p in parts)
    arrays = [array for part in parts for array in part] + list(extra)
    channels = arrays[0].shape[0]
    width = taps.shape[0]
    block = min(channels, 256)
    row = lambda n: pl.BlockSpec((block, n), lambda i: (i, 0))
    return pl.pallas_call(
        functools.partial(kernel, counts),
        out_shape=[jax.ShapeDtypeStruct((channels, n), BF16) for n in widths],
        grid=(channels // block,),
        in_specs=[row(array.shape[1]) for array in arrays]
        + [pl.BlockSpec((width, block), lambda i: (0, i))]
        + [whole(t.shape) for t in tables],
        out_specs=[row(n) for n in widths],
        compiler_params=grant(10),
    )(*arrays, taps, *tables)


def ring(block, axis, distance):
    count = lax.axis_size(axis)
    if distance == 0:
        return block
    return lax.ppermute(block, axis, [(i, (i + distance) % count) for i in range(count)])


def forward(block, axis):
    count = lax.axis_size(axis)
    return lax.ppermute(block, axis, [(i, i + 1) for i in range(count - 1)])


def swapped(block, axis, bit):
    return lax.ppermute(block, axis, [(i, i ^ bit) for i in range(lax.axis_size(axis))])


def neighbour_weights(ids, out_weight, width, groups, chunks):
    slabs = turned(
        ids,
        out_weight,
        width,
        (lambda ids: ids[1] ^ 1 ^ ((ids[0] & 1) * 2), lambda ids: ids[1] ^ 2 ^ (ids[0] & 1)),
        groups,
        chunks,
    )
    return [swapped(slabs[0], "tp", 1), swapped(slabs[1], "tp", 2)]


def both_cores(sides, after):
    held = lax.optimization_barrier((*sides, after))
    out = []
    for straight in held[:2]:
        out.append((straight, swapped(straight, "ctx", 1)))
    return out, held[2]


def neighbours(gated):
    return [swapped(gated[0], "tp", 1), swapped(gated[1], "tp", 2)]


def shards(query_proj, key_proj, value_proj, short_taps, long_filter, out_weight, medium_taps):
    channels, tokens = query_proj.shape
    groups = lax.axis_size("ctx")
    length = long_filter.shape[1]
    tables = long_tables(length, groups)
    ids = jnp.stack([lax.axis_index("ctx"), lax.axis_index("tp")]).astype(jnp.int32)
    edges = forward(tails((query_proj, key_proj, value_proj)), "ctx").astype(F32)
    aux = jnp.concatenate([short_taps.reshape(9, channels), edges[:7]], axis=0).T
    owned = long_filter.shape[0]
    four = lax.axis_size("tp") == 4
    chunks = 2 if four and owned % 32 == 0 else 1
    rows = owned // chunks
    spec = spectra(long_filter, tables, min(owned, 16))
    sent = []
    for c in range(chunks):
        cuts = (0, groups // 2, groups) if c == 0 else (0, groups)
        made = []
        for first, end in zip(cuts, cuts[1:]):
            made += mix(ids, key_proj, value_proj, aux, groups, c, chunks, first, end - first)
        sent.append(made)
    sides, weights = None, None
    if four:
        part = out_weight.shape[1] // 4
        held = lax.optimization_barrier((out_weight, sent[-1][0]))
        sent[-1][0] = held[1]
        sides = neighbour_weights(ids, held[0], part, groups, chunks)
        weights = turned(
            ids,
            held[0],
            part,
            (lambda ids: ids[1], lambda ids: ids[1] ^ 1, lambda ids: ids[1] ^ 2),
            groups,
            chunks,
        )
    query = query_conv(query_proj, aux)
    count = tokens // LANES
    half_tiles = count // 2
    own = {0: [], 1: []}
    near = {0: [], 1: []}
    for c in range(chunks):
        last = c == chunks - 1
        got = []
        for s, piece in enumerate(sent[c]):
            got.append(ring(piece, "ctx", s))
        runs = (half_tiles, half_tiles) if last else (count,)
        results = list(long_conv(ids, got, spec, tables, min(rows, 32), runs, c * rows))
        for h in (1, 0) if last else (None,):
            back = [
                ring(piece, "ctx", s)
                for s, piece in enumerate(results[h::2] if last else results)
            ]
            start = h * half_tiles if last else 0
            gated = list(gate(ids, back, query, c, chunks, start, half_tiles))
            if four and c == 0 and h != 0:
                sides, gated[0] = both_cores(sides, gated[0])
            beside = neighbours(gated) if four else None
            for at in (h,) if last else (0, 1):
                own[at].append(gated)
                near[at].append(beside)
    parts = {}
    for h in (1, 0):
        if not four:
            source = jnp.concatenate(own[h][0], axis=1)
            partial = lax.dot_general(
                out_weight, source, (((0,), (0,)), ((), ())), preferred_element_type=F32
            ).astype(BF16)
            parts[h] = [[lax.psum_scatter(partial, "tp", scatter_dimension=0, tiled=True)]]
            continue
        sources = list(zip(own[h], near[h]))
        send = project(ids, sources, (weights[2], weights[1]), sides, 1, h)
        got = [swapped(send[0], "tp", 2), swapped(send[1], "tp", 1)]
        keep = project(ids, sources, (weights[0], weights[0]), sides, 0, h)
        parts[h] = [[keep[0], got[0]], [keep[1], got[1]]]
    width = medium_taps.shape[0]
    half = tokens // 2
    tables = medium_tables(width)
    later, edge, tail = medium_call(
        late_kernel, parts[1], (), medium_taps, tables, (half, width, half - width)
    )
    edge = forward(edge, "ctx")
    return tuple(
        medium_call(
            early_kernel, parts[0], (edge, later, tail), medium_taps, tables, (tokens, tokens)
        )
    )


def solution(mesh):
    in_specs = (
        P("tp", "ctx"),
        P("tp", "ctx"),
        P("tp", "ctx"),
        P(None, None, "tp"),
        P(("tp", "ctx"), None),
        P("tp", None),
        P(None, "tp"),
    )
    out_specs = (P("tp", "ctx"), P("tp", "ctx"))
    return jax.shard_map(shards, mesh=mesh, in_specs=in_specs, out_specs=out_specs, check_vma=False)
```
